32 devices in a mesh: shot: 8 (over z, x), lag: 4 (over y, core).
Axes of the slice: x: 2, y: 2, z: 4, core: 2. Of those that a mesh axis runs over, the one named last changes fastest.
Arguments:
- traces: bfloat16 [48, 256, 8192], P('shot', 'lag'), may hold values from -64 to 64, as said below
- live_mask: int32 [48, 256], P('shot', 'lag'), may hold values 0 or 1
- gap_samples: int32 [1], replicated, may hold values from 1 to 32
Outputs:
- residual_traces: bfloat16 [48, 256, 8192], P('shot', 'lag')
The draws below stay inside these ranges and needn't reach their ends.
Inputs may be any that keep to these rules, and one draw needn't show every extreme that they name: `traces`: recorded samples.
All inputs are finite; a program needn't handle non-finite values. No bound on the sum of `live_mask` on one device may be relied on, other than what follows from the above.
Results may differ from the reference program's by a relative error of at most 0.015.
The reference program's roundings to bfloat16 on the way (of `table`, `spectra`, `rotated`, `filter_bf` and `error`) count: a program that leaves them out, or rounds other values in their place, can miss the bound.
Values may be sent and summed in bfloat16 or wider, within the bound.
A program may use at most 128 MiB of HBM per device.

```python
import jax
import jax.numpy as jnp
from jax import lax

CHANNELS = 256
SAMPLES = 8192
LAGS = 4
FREQS = 512
CORR_LAGS = 8
SHOTS = 48


def draw_traces(key, part):
    subkeys = jax.random.split(jax.random.fold_in(key, 7), 8)
    source_count = 128
    noise_part = 0.3 * jax.random.normal(subkeys[0], (SHOTS, CHANNELS, SAMPLES), jnp.float32)
    band_edge = jnp.pi * FREQS / SAMPLES
    centre = band_edge * jax.random.uniform(subkeys[1], (source_count,), jnp.float32, 0.15, 0.95)
    radius = jax.random.uniform(subkeys[2], (source_count,), jnp.float32, 0.96, 0.995)
    first_coef = 2.0 * radius * jnp.cos(centre)
    second_coef = -radius * radius
    variance = (1.0 + radius * radius) / ((1.0 - radius * radius) * ((1.0 + radius * radius) ** 2 - first_coef * first_coef))
    drive_scale = 1.0 / jnp.sqrt(variance)

    def advance(carry, sample_idx):
        earlier, latest = carry
        innovation = jax.random.normal(jax.random.fold_in(subkeys[3], sample_idx), (SHOTS, source_count), jnp.float32)
        updated = first_coef * latest + second_coef * earlier + drive_scale * innovation
        return ((latest, updated), updated)
    start_state = (jnp.zeros((SHOTS, source_count), jnp.float32), jnp.zeros((SHOTS, source_count), jnp.float32))
    final_state, sources = lax.scan(advance, start_state, jnp.arange(SAMPLES, dtype=jnp.int32))
    amplitude = jnp.exp(-3.0 * jnp.log(10.0) * jax.random.uniform(subkeys[4], (source_count,), jnp.float32))
    mixing = jax.random.normal(subkeys[5], (CHANNELS, source_count), jnp.float32) * (0.3 * amplitude)[None, :]
    shot_ramp = 3.0 ** (jnp.arange(SHOTS, dtype=jnp.float32) / max(SHOTS - 1, 1))
    chan_scale = jnp.exp(jax.random.uniform(subkeys[6], (CHANNELS,), jnp.float32, jnp.log(0.5), jnp.log(5.0)))
    trace_scale = jax.random.uniform(subkeys[7], (SHOTS, CHANNELS), jnp.float32, 0.7, 1.3) * chan_scale[None, :]
    coherent = jnp.einsum('tsm,cm->sct', sources, mixing)
    recorded = (noise_part + coherent) * trace_scale[:, :, None] * shot_ramp[:, None, None]
    return jnp.clip(recorded, -64.0, 64.0).astype(jnp.bfloat16)


def set_ends(result, stream_key, low, largest):
    longest = result.shape.index(max(result.shape))
    spots = []
    for shift in (0, 1):
        where = [jax.random.randint(jax.random.fold_in(stream_key, axis), (), 0, length) for axis, length in enumerate(result.shape)]
        where[longest] = (where[longest] + shift) % result.shape[longest]
        spots.append(tuple(where))
    return result.at[spots[0]].set(low).at[spots[1]].set(largest)


def setup_inputs(seed: int = 0) -> dict:
    arg_keys = jax.random.split(jax.random.key(seed), 4)
    traces = draw_traces(jax.random.fold_in(arg_keys[3], 71), 0)
    live_mask = set_ends((jax.random.randint(arg_keys[1], (SHOTS, CHANNELS), 0, 8) < 7).astype(jnp.int32), jax.random.fold_in(arg_keys[1], 1), 0, 1)
    gap_samples = jax.random.randint(arg_keys[2], (1,), 1, 33).astype(jnp.int32)
    return {"traces": traces, "live_mask": live_mask, "gap_samples": gap_samples}


def dft_table(first_row, row_count, samples, band_size):
    times_idx = jnp.arange(row_count, dtype=jnp.int32) + first_row
    harmonic = jnp.arange(1, band_size + 1, dtype=jnp.int32)
    phase = times_idx[:, None] * harmonic[None, :] % (2 * samples)
    angle = phase.astype(jnp.float32) * (jnp.pi / samples)
    return jnp.concatenate([jnp.cos(angle), jnp.sin(angle)], axis=1).astype(jnp.bfloat16)

def delay_tables(delays, samples, band_size):
    harmonic = jnp.arange(1, band_size + 1, dtype=jnp.int32)
    phase = delays[:, None] * harmonic[None, :] % (2 * samples)
    angle = phase.astype(jnp.float32) * (jnp.pi / samples)
    return (jnp.cos(angle), jnp.sin(angle))

def delay_apply(spectrum, cosine, sine):
    band_size = cosine.shape[-1]
    real_part = spectrum[..., :band_size]
    imag_part = spectrum[..., band_size:]
    return jnp.concatenate([real_part * cosine - imag_part * sine, imag_part * cosine + real_part * sine], axis=-1)

def reference(traces, live_mask, gap_samples):
    table = dft_table(0, SAMPLES, SAMPLES, FREQS)
    spacing = SAMPLES // (2 * FREQS)
    tap_delays = jnp.arange(LAGS, dtype=jnp.int32) * spacing
    lag_list = jnp.concatenate([tap_delays, gap_samples[0].astype(jnp.int32) + tap_delays])
    cosine, sine = delay_tables(lag_list, SAMPLES, FREQS)
    live_bf = live_mask.astype(jnp.bfloat16)

    def spectrum_of(shot_idx):
        masked = traces[shot_idx] * live_bf[shot_idx][:, None]
        return jnp.dot(masked.astype(jnp.float32), table.astype(jnp.float32), preferred_element_type=jnp.float32).astype(jnp.bfloat16)
    spectra = lax.map(spectrum_of, jnp.arange(SHOTS, dtype=jnp.int32))

    def accumulate(carry, spectrum):
        rotated = delay_apply(spectrum.astype(jnp.float32)[None], cosine[:, None, :], sine[:, None, :]).astype(jnp.bfloat16)
        update = jnp.einsum('kaf,bf->kab', rotated.astype(jnp.float32), spectrum.astype(jnp.float32))
        return (carry + update, None)
    start_sum = jnp.zeros((CORR_LAGS, CHANNELS, CHANNELS), jnp.float32)
    summed, unused = lax.scan(accumulate, start_sum, spectra)
    correlation = summed * (1.0 / SAMPLES) * (1.0 / (SAMPLES * SHOTS))
    whiten = 0.1 * jnp.mean(jnp.diagonal(correlation[0])) + 1e-06
    zero_lag = correlation[0] + whiten * jnp.eye(CHANNELS, dtype=jnp.float32)
    weighted = jnp.concatenate([zero_lag[None], correlation[1:]], axis=0)
    blocks = []
    for row_block in range(LAGS):
        row_parts = []
        for col_block in range(LAGS):
            if row_block >= col_block:
                row_parts.append(weighted[row_block - col_block])
            else:
                row_parts.append(weighted[col_block - row_block].T)
        blocks.append(jnp.concatenate(row_parts, axis=1))
    system = jnp.concatenate(blocks, axis=0)
    rhs = jnp.concatenate([weighted[LAGS + row_block] for row_block in range(LAGS)], axis=0)
    lower_factor = jnp.linalg.cholesky(system)
    filter_all = jax.scipy.linalg.cho_solve((lower_factor, True), rhs)
    filter_bf = filter_all.astype(jnp.bfloat16).reshape(LAGS, CHANNELS, CHANNELS)

    def residual_of(shot_idx):
        spectrum = spectra[shot_idx]
        mixed = jnp.einsum('jab,af->jbf', filter_bf.astype(jnp.float32), spectrum.astype(jnp.float32))
        shifted = delay_apply(mixed, cosine[LAGS:, None, :], sine[LAGS:, None, :])
        error = (spectrum.astype(jnp.float32) - jnp.sum(shifted, axis=0)).astype(jnp.bfloat16)
        restored = jnp.dot(error.astype(jnp.float32), table.T.astype(jnp.float32), preferred_element_type=jnp.float32)
        return (restored * (1.0 / SAMPLES) * live_bf[shot_idx].astype(jnp.float32)[:, None]).astype(jnp.bfloat16)
    return lax.map(residual_of, jnp.arange(SHOTS, dtype=jnp.int32))
```

```python
import functools

import jax
import jax.numpy as jnp
import ml_dtypes
import numpy as np
from jax import lax
from jax.experimental import pallas as pl
from jax.experimental.pallas import tpu as pltpu
from jax.sharding import PartitionSpec as P

LAGS=4
HALF=128
PIVOTS=4

def mm(a, b, dims=((1,), (0,))):
    return lax.dot_general(a, b, (dims, ((), ())), precision=lax.Precision.HIGHEST, preferred_element_type=jnp.float32)


def factor_half(mat):
    lane = lax.broadcasted_iota(jnp.int32, (8, HALF), 1)
    row = lax.broadcasted_iota(jnp.int32, (8, HALF), 0)
    count = HALF // 8
    tiles = [mat[8 * t : 8 * t + 8, :] for t in range(count)]

    def spread(x):
        return jnp.broadcast_to(x, (8, HALF))

    def reduce_by(p, inv, x):
        done = []
        for j in range(PIVOTS):
            value = x[j]
            for i in range(j):
                value = value - p[i, j] * done[i]
            done.append(value * inv[j])
        return done

    for k in range(0, HALF, PIVOTS):
        home, off = k // 8, k % 8
        rows = [spread(tiles[home][off + i : off + i + 1, :]) for i in range(PIVOTS)]
        p = {(i, j): spread(rows[i][:, k + j : k + j + 1]) for i in range(PIVOTS) for j in range(i, PIVOTS)}
        inside = (lane >= k) & (lane < k + PIVOTS)
        rows = [jnp.where(inside, jnp.where(lane == k + i, 1.0, 0.0), rows[i]) for i in range(PIVOTS)]
        inv = []
        for i in range(PIVOTS):
            for m in range(i):
                for j in range(i, PIVOTS):
                    if m == i - 1:
                        p[i, j] = p[i, j] - p[m, i] * p[m, j]
            inv.append(lax.rsqrt(p[i, i]))
            for j in range(i + 1, PIVOTS):
                p[i, j] = p[i, j] * inv[i]
            for l in range(i + 2, PIVOTS):
                for j in range(l, PIVOTS):
                    p[l, j] = p[l, j] - p[i, l] * p[i, j]
        w = reduce_by(p, inv, rows)
        for t in range(home, count):
            if t == home and off + PIVOTS == 8:
                updated = tiles[t]
            else:
                c = reduce_by(p, inv, [spread(tiles[t][:, k + j : k + j + 1]) for j in range(PIVOTS)])
                kept = jnp.where(inside, 0.0, tiles[t])
                updated = kept - ((c[0] * w[0] + c[1] * w[1]) + (c[2] * w[2] + c[3] * w[3]))
            if t == home:
                updated = jnp.where(row < off, tiles[t], updated)
                for i in range(PIVOTS):
                    updated = jnp.where(row == off + i, w[i], updated)
            tiles[t] = updated
    return jnp.concatenate(
        [jnp.where(lane <= row + 8 * t, tiles[t], 0.0) for t in range(count)], axis=0
    )


def solve_kernel(corr_ref, rhs_ref, out_ref, aug, diag, first_inv, coupling):
    channels = corr_ref.shape[1]
    order = LAGS * channels
    width = aug.shape[1]
    block = 2 * HALF
    count = order // block
    local = rhs_ref.shape[1]

    for lag in range(LAGS):
        value = corr_ref[lag]
        if lag == 0:
            same = lax.broadcasted_iota(jnp.int32, value.shape, 0) == lax.broadcasted_iota(jnp.int32, value.shape, 1)
            trace = jnp.sum(jnp.where(same, value, 0.0))
            value = value + jnp.where(same, 0.1 * (trace / channels) + 1e-06, 0.0)
        else:
            flipped = value.T
        for low in range(LAGS - lag):
            high = low + lag
            rows, cols = low * channels, high * channels
            aug[rows : rows + channels, cols : cols + channels] = value if lag == 0 else flipped
    aug[:, order:] = jnp.zeros((order, width - order), jnp.float32)
    for tap in range(LAGS):
        aug[tap * channels : (tap + 1) * channels, order : order + local] = rhs_ref[tap].T
    diag[...] = aug[:HALF, :HALF]

    def step(half_step, carry):
        diag[...] = factor_half(diag[...])
        for b in range(count):
            o = b * block
            mid, end = o + HALF, o + block

            @pl.when(half_step == 2 * b)
            def _():
                low = mm(aug[mid:end, o:mid], diag[...], ((1,), (1,)))
                first_inv[...] = diag[...]
                coupling[...] = low
                diag[...] = aug[mid:end, mid:end] - mm(low, low, ((1,), (1,)))

            @pl.when(half_step == 2 * b + 1)
            def _():
                top, last = first_inv[...], diag[...]
                corner = -mm(last, mm(coupling[...], top))
                aug[o:mid, o:mid] = top
                aug[o:mid, mid:end] = jnp.zeros((HALF, HALF), jnp.float32)
                aug[mid:end, o:mid] = corner
                aug[mid:end, mid:end] = last
                for c in range(end, width, block):
                    ce = min(c + block, width)
                    aug[o:end, c:ce] = mm(aug[o:end, o:end], aug[o:end, c:ce])
                for r in range(end, order, block):
                    left = aug[o:end, r : r + block]
                    for c in range(r, width, block):
                        ce = min(c + block, width)
                        aug[r : r + block, c:ce] = aug[r : r + block, c:ce] - mm(left, aug[o:end, c:ce], ((0,), (0,)))
                if end < order:
                    diag[...] = aug[end : end + HALF, end : end + HALF]

        return carry

    lax.fori_loop(0, 2 * count, step, 0)
    for b in range(count - 1, -1, -1):
        o, end = b * block, (b + 1) * block
        known = aug[o:end, order:]
        if end < order:
            known = known - mm(aug[o:end, end:order], aug[end:order, order:])
        aug[o:end, order:] = mm(aug[o:end, o:end], known, ((0,), (0,)))
    out_ref[...] = aug[:, order : order + local].T.astype(jnp.bfloat16)


def solve(corr, rhs):
    channels = corr.shape[1]
    local = rhs.shape[1]
    order = LAGS * channels
    width = order + HALF * pl.cdiv(local, HALF)
    vm = pl.BlockSpec(memory_space=pltpu.VMEM)
    return pl.pallas_call(
        solve_kernel,
        out_shape=jax.ShapeDtypeStruct((local, order), jnp.bfloat16),
        in_specs=[vm, vm],
        out_specs=vm,
        scratch_shapes=[
            pltpu.VMEM((order, width), jnp.float32),
            pltpu.VMEM((HALF, HALF), jnp.float32),
            pltpu.VMEM((HALF, HALF), jnp.float32),
            pltpu.VMEM((HALF, HALF), jnp.float32),
        ],
        compiler_params=pltpu.CompilerParams(vmem_limit_bytes=40 << 20),
        name="block_solve",
    )(corr, rhs)


MESH = pl.DeviceIdType.MESH
FINE = 128


def dft_table(samples, band_size):
    times = np.arange(samples, dtype=np.int64)
    harmonic = np.arange(1, band_size + 1, dtype=np.int64)
    phase = (times[:, None] * harmonic[None, :]) % (2 * samples)
    circle = np.arange(2 * samples).astype(np.float32) * np.float32(np.pi / samples)
    cosines = np.cos(circle.astype(np.float64)).astype(np.float32).astype(ml_dtypes.bfloat16)[phase]
    sines = np.sin(circle.astype(np.float64)).astype(np.float32).astype(ml_dtypes.bfloat16)[phase]
    pair = np.stack([cosines.reshape(samples, -1, FINE), sines.reshape(samples, -1, FINE)], axis=2)
    return pair.reshape(samples, 2 * band_size)


def low_bit(value):
    return value & -value


def front_kernel(
    shape, scales, x_hbm, table_hbm, live_ref, cos_ref, sin_ref, all_ref, sys_ref, rhs_ref,
    x_v, tab_v, rot_v, acc_v, part_v, recv_v, full_v, rfull_v,
    x_sem, tab_sem, spec_send, spec_recv, red_send, red_recv, piece_send, piece_recv, lag_send, lag_recv,
):
    shots, shot_shards, lag_shards = shape
    rows, samples = x_v.shape
    local = rows // shots
    chunks = all_ref.shape[0]
    wide = 2 * FINE
    block = samples // x_sem.shape[0]
    my_shot, my_lag = lax.axis_index("shot"), lax.axis_index("lag")
    bits = [1 << i for i in range(lag_shards.bit_length() - 2, -1, -1)]

    def x_copy(b):
        span = pl.ds(b * block, block)
        return pltpu.make_async_copy(x_hbm.at[:, span], x_v.at[:, span], x_sem.at[b])

    def first_copy(b):
        span = pl.ds(b * block, block)
        return pltpu.make_async_copy(
            table_hbm.at[span, pl.ds(0, wide)], tab_v.at[0, span], tab_sem.at[chunks + b]
        )

    def table_copy(c):
        return pltpu.make_async_copy(
            table_hbm.at[:, pl.ds(c * wide, wide)], tab_v.at[c], tab_sem.at[c]
        )

    blocks = x_sem.shape[0]
    for b in range(blocks):
        x_copy(b).start()
        first_copy(b).start()
    for c in range(1, chunks):
        table_copy(c).start()

    barrier = pltpu.get_barrier_semaphore()
    for j in range(1, shot_shards):
        pl.semaphore_signal(barrier, inc=1, device_id=(my_shot ^ j, my_lag), device_id_type=MESH)
    for v in bits:
        pl.semaphore_signal(barrier, inc=1, device_id=(my_shot, my_lag ^ v), device_id_type=MESH)

    def own_rows(lag):
        return pl.ds(pl.multiple_of(lag * local, local), local)

    def spec_copy(c, delta):
        v = low_bit(delta)
        span = own_rows(my_lag ^ (delta ^ v))
        return pltpu.make_async_remote_copy(
            src_ref=all_ref.at[c, span], dst_ref=all_ref.at[c, span],
            send_sem=spec_send.at[c, delta], recv_sem=spec_recv.at[c, delta],
            device_id=(my_shot, my_lag ^ v), device_id_type=MESH,
        )

    def spec_arrival(c, delta):
        v = low_bit(delta)
        span = own_rows(my_lag ^ delta)
        return pltpu.make_async_remote_copy(
            src_ref=all_ref.at[c, span], dst_ref=all_ref.at[c, span],
            send_sem=spec_send.at[c, delta], recv_sem=spec_recv.at[c, delta],
            device_id=(my_shot, my_lag ^ v), device_id_type=MESH,
        )

    def transform(c, loaded):
        total = None
        for b in range(blocks):
            if loaded is not None:
                loaded(b)
            term = jnp.dot(
                x_v[:, b * block : (b + 1) * block], tab_v[c, b * block : (b + 1) * block, :],
                preferred_element_type=jnp.float32,
            )
            total = term if total is None else total + term
        value = (total * live_ref[...]).astype(jnp.bfloat16)
        for s in range(shots):
            all_ref[c, own_rows(my_lag), s * wide : (s + 1) * wide] = value[s * local : (s + 1) * local]

    def send_own(c):
        for v in bits:
            spec_copy(c, v).start()

    def first_loaded(b):
        x_copy(b).wait()
        first_copy(b).wait()

    transform(0, first_loaded)
    pl.semaphore_wait(barrier, shot_shards - 1 + len(bits))
    send_own(0)

    def transform_step(c, carry):
        table_copy(c).wait()
        transform(c, None)
        send_own(c)
        return carry

    lax.fori_loop(1, chunks, transform_step, 0)
    acc_v[...] = jnp.zeros_like(acc_v)
    deltas = sorted(range(1, lag_shards), key=lambda d: -low_bit(d))

    def correlate_step(c, carry):
        for delta in deltas:
            if low_bit(delta) > 1:
                spec_arrival(c, delta).wait_recv()
                for v in bits:
                    if v < low_bit(delta):
                        spec_copy(c, delta | v).start()
        own = all_ref[c, own_rows(my_lag), :].astype(jnp.float32)
        for k in range(2 * LAGS):
            cosine, sine = cos_ref[c, k : k + 1, :], sin_ref[c, k : k + 1, :]
            for s in range(shots):
                o = s * wide
                real, imag = own[:, o : o + FINE], own[:, o + FINE : o + wide]
                rot_v[k * local : (k + 1) * local, o : o + FINE] = (real * cosine - imag * sine).astype(jnp.bfloat16)
                rot_v[k * local : (k + 1) * local, o + FINE : o + wide] = (imag * cosine + real * sine).astype(jnp.bfloat16)
        for delta in deltas:
            if low_bit(delta) == 1:
                spec_arrival(c, delta).wait_recv()
        acc_v[...] = acc_v[...] + lax.dot_general(
            rot_v[...], all_ref[c], (((1,), (1,)), ((), ())), preferred_element_type=jnp.float32
        )
        return carry

    lax.fori_loop(0, chunks, correlate_step, 0)

    half_rows = LAGS * local
    piece = part_v.shape[2]
    for h in range(2):
        for p in range(shot_shards):
            top, lane = h * half_rows + (p // 2) * piece, (p % 2) * FINE
            part_v[h, p] = acc_v[top : top + piece, lane : lane + FINE]

    def reduce_copy(h, j):
        return pltpu.make_async_remote_copy(
            src_ref=part_v.at[h, my_shot ^ j], dst_ref=recv_v.at[h, j],
            send_sem=red_send.at[h, j], recv_sem=red_recv.at[h, j],
            device_id=(my_shot ^ j, my_lag), device_id_type=MESH,
        )

    for h in range(2):
        for j in range(1, shot_shards):
            reduce_copy(h, j).start()

    def piece_copy(h, j, owner):
        ref = full_v.at[my_lag, owner] if h == 0 else rfull_v.at[owner]
        return pltpu.make_async_remote_copy(
            src_ref=ref, dst_ref=ref,
            send_sem=piece_send.at[h, j], recv_sem=piece_recv.at[h, j],
            device_id=(my_shot ^ j, my_lag), device_id_type=MESH,
        )

    def lag_copy(j, delta, arriving):
        v = low_bit(delta)
        ref = full_v.at[my_lag ^ (delta if arriving else delta ^ v), my_shot ^ j]
        return pltpu.make_async_remote_copy(
            src_ref=ref, dst_ref=ref,
            send_sem=lag_send.at[j, delta], recv_sem=lag_recv.at[j, delta],
            device_id=(my_shot, my_lag ^ v), device_id_type=MESH,
        )

    def reduce(h):
        total = part_v[h, my_shot]
        for j in range(1, shot_shards):
            reduce_copy(h, j).wait_recv()
            total = total + recv_v[h, j]
        total = total * scales[0] * scales[1]
        if h == 0:
            full_v[my_lag, my_shot] = total
        else:
            rfull_v[my_shot] = total
        for j in range(1, shot_shards):
            piece_copy(h, j, my_shot).start()

    reduce(0)
    for v in bits:
        lag_copy(0, v, False).start()
    reduce(1)
    for j in range(1, shot_shards):
        piece_copy(0, j, my_shot ^ j).wait_recv()
        for v in bits:
            lag_copy(j, v, False).start()
    for j in range(shot_shards):
        for delta in deltas:
            if low_bit(delta) > 1:
                lag_copy(j, delta, True).wait_recv()
                for v in bits:
                    if v < low_bit(delta):
                        lag_copy(j, delta | v, False).start()
    unit = min(piece, local)
    for j in range(1, shot_shards):
        piece_copy(1, j, my_shot ^ j).wait_recv()
    for p in range(shot_shards):
        for r in range(0, piece, unit):
            row, lane = (p // 2) * piece + r, (p % 2) * FINE
            k, a = row // local, row % local
            rhs_ref[k, a : a + unit, lane : lane + FINE] = rfull_v[p, r : r + unit]
    for j in range(shot_shards):
        for delta in deltas:
            if low_bit(delta) == 1:
                lag_copy(j, delta, True).wait_recv()
    for q in range(lag_shards):
        for p in range(shot_shards):
            for r in range(0, piece, unit):
                row, lane = (p // 2) * piece + r, (p % 2) * FINE
                k, a = row // local, row % local + q * local
                sys_ref[k, a : a + unit, lane : lane + FINE] = full_v[q, p, r : r + unit]
    for c in range(chunks):
        for delta in deltas:
            spec_copy(c, delta).wait_send()
    for h in range(2):
        for j in range(1, shot_shards):
            reduce_copy(h, j).wait_send()
            piece_copy(h, j, my_shot).wait_send()
    for j in range(shot_shards):
        for delta in deltas:
            lag_copy(j, delta, False).wait_send()


def front(traces, table, live, cosine, sine, shot_shards, lag_shards):
    shots, local, samples = traces.shape
    rows = shots * local
    width = table.shape[1]
    chunks = width // (2 * FINE)
    channels = local * lag_shards
    blocks = 4
    piece = 2 * LAGS * local // shot_shards
    total_shots = shots * shot_shards
    scales = (1.0 / samples, 1.0 / (samples * total_shots))
    hbm = pl.BlockSpec(memory_space=pl.ANY)
    vm = pl.BlockSpec(memory_space=pltpu.VMEM)
    sem = pltpu.SemaphoreType.DMA
    return pl.pallas_call(
        functools.partial(front_kernel, (shots, shot_shards, lag_shards), scales),
        out_shape=(
            jax.ShapeDtypeStruct((chunks, channels, shots * 2 * FINE), jnp.bfloat16),
            jax.ShapeDtypeStruct((LAGS, channels, channels), jnp.float32),
            jax.ShapeDtypeStruct((LAGS, local, channels), jnp.float32),
        ),
        in_specs=[hbm, hbm, vm, vm, vm],
        out_specs=(vm, vm, vm),
        scratch_shapes=[
            pltpu.VMEM((rows, samples), jnp.bfloat16),
            pltpu.VMEM((chunks, samples, 2 * FINE), jnp.bfloat16),
            pltpu.VMEM((2 * LAGS * local, shots * 2 * FINE), jnp.bfloat16),
            pltpu.VMEM((2 * LAGS * local, channels), jnp.float32),
            pltpu.VMEM((2, shot_shards, piece, FINE), jnp.float32),
            pltpu.VMEM((2, shot_shards, piece, FINE), jnp.float32),
            pltpu.VMEM((lag_shards, shot_shards, piece, FINE), jnp.float32),
            pltpu.VMEM((shot_shards, piece, FINE), jnp.float32),
            sem((blocks,)),
            sem((chunks + blocks,)),
            sem((chunks, lag_shards)),
            sem((chunks, lag_shards)),
            sem((2, shot_shards)),
            sem((2, shot_shards)),
            sem((2, shot_shards)),
            sem((2, shot_shards)),
            sem((shot_shards, lag_shards)),
            sem((shot_shards, lag_shards)),
        ],
        compiler_params=pltpu.CompilerParams(
            collective_id=0, has_side_effects=True, vmem_limit_bytes=50 << 20
        ),
        name="front",
    )(traces.reshape(rows, samples), table, live, cosine, sine)


def tail_kernel(shots, scale, all_ref, filter_ref, cos_ref, sin_ref, live_ref, table_ref, out_ref, err_v):
    chunks = all_ref.shape[0]
    local = filter_ref.shape[0]
    channels = all_ref.shape[1]
    wide = 2 * FINE
    my_lag = lax.axis_index("lag")

    @pl.when(pl.program_id(0) == 0)
    def _():
        taps = jnp.concatenate(
            [filter_ref[:, j * channels : (j + 1) * channels] for j in range(LAGS)], axis=0
        )

        def chunk_step(c, carry):
            own = all_ref[c, pl.ds(pl.multiple_of(my_lag * local, local), local), :].astype(jnp.float32)
            mixed = jnp.dot(taps, all_ref[c], preferred_element_type=jnp.float32)
            for s in range(shots):
                o = s * wide
                real, imag = own[:, o : o + FINE], own[:, o + FINE : o + wide]
                for j in range(LAGS):
                    cosine, sine = cos_ref[c, LAGS + j : LAGS + j + 1, :], sin_ref[c, LAGS + j : LAGS + j + 1, :]
                    a = mixed[j * local : (j + 1) * local, o : o + FINE]
                    b = mixed[j * local : (j + 1) * local, o + FINE : o + wide]
                    real = real - (a * cosine - b * sine)
                    imag = imag - (b * cosine + a * sine)
                err_v[c, s * local : (s + 1) * local, :FINE] = real.astype(jnp.bfloat16)
                err_v[c, s * local : (s + 1) * local, FINE:] = imag.astype(jnp.bfloat16)
            return carry

        lax.fori_loop(0, chunks, chunk_step, 0)

    error = jnp.concatenate([err_v[c] for c in range(chunks)], axis=1)
    value = lax.dot_general(
        error, table_ref[...], (((1,), (1,)), ((), ())), preferred_element_type=jnp.float32
    )
    out_ref[...] = (value * scale * live_ref[...]).astype(jnp.bfloat16)


def tail(all_spec, filter_rows, cosine, sine, live, table, shots):
    samples, depth = table.shape
    rows = live.shape[0]
    step = min(1024, samples)

    def whole(array):
        return pl.BlockSpec(array.shape, lambda t: (0,) * array.ndim)

    return pl.pallas_call(
        functools.partial(tail_kernel, shots, 1.0 / samples),
        out_shape=jax.ShapeDtypeStruct((rows, samples), jnp.bfloat16),
        grid=(samples // step,),
        in_specs=[
            whole(all_spec), whole(filter_rows), whole(cosine), whole(sine), whole(live),
            pl.BlockSpec((step, depth), lambda t: (t, 0)),
        ],
        out_specs=pl.BlockSpec((rows, step), lambda t: (0, t)),
        scratch_shapes=[pltpu.VMEM((depth // (2 * FINE), rows, 2 * FINE), jnp.bfloat16)],
        compiler_params=pltpu.CompilerParams(vmem_limit_bytes=40 << 20),
        name="tail",
    )(all_spec, filter_rows, cosine, sine, live, table)


def delay_tables(delays, samples, band_size):
    harmonic = jnp.arange(1, band_size + 1, dtype=jnp.int32)
    phase = delays[:, None] * harmonic[None, :] % (2 * samples)
    angle = phase.astype(jnp.float32) * (jnp.pi / samples)
    return (jnp.cos(angle), jnp.sin(angle))


def shards(traces, live_mask, gap_samples):
    shot_count, local_chan, samples = traces.shape
    band_size = samples // 16
    shot_shards, lag_shards = lax.axis_size("shot"), lax.axis_size("lag")
    table = jnp.asarray(dft_table(samples, band_size))
    rows = shot_count * local_chan
    live = live_mask.astype(jnp.float32).reshape(rows, 1)
    spacing = samples // (2 * band_size)
    tap_delays = jnp.arange(LAGS, dtype=jnp.int32) * spacing
    lag_list = jnp.concatenate([tap_delays, gap_samples[0] + tap_delays])
    cosine, sine = delay_tables(lag_list, samples, band_size)

    def by_chunk(x):
        return x.reshape(2 * LAGS, band_size // FINE, FINE).transpose(1, 0, 2)

    cosine, sine = by_chunk(cosine), by_chunk(sine)
    turn = jnp.where(jnp.arange(2 * LAGS) < LAGS, 1.0, -1.0)[None, :, None]
    all_spec, system, rhs = front(traces, table, live, cosine, sine * turn, shot_shards, lag_shards)
    filter_rows = solve(system, rhs)
    restored = tail(all_spec, filter_rows, cosine, sine, live, table, shot_count)
    return restored.reshape(shot_count, local_chan, samples)


def solution(mesh):
    placed = (P("shot", "lag", None), P("shot", "lag"), P())
    return jax.shard_map(
        shards, mesh=mesh, in_specs=placed, out_specs=P("shot", "lag", None), check_vma=False
    )
```

```python
import functools

import jax
import jax.numpy as jnp
import ml_dtypes
import numpy as np
from jax import lax
from jax.experimental import pallas as pl
from jax.experimental.pallas import tpu as pltpu
from jax.sharding import PartitionSpec as P

LAGS=4
HALF=128
STEP=8

def mm(a, b, dims=((1,), (0,))):
    return lax.dot_general(a, b, (dims, ((), ())), precision=lax.Precision.HIGHEST, preferred_element_type=jnp.float32)


def spread(x):
    return jnp.broadcast_to(x, (STEP, HALF))


def lane_columns(tile, first):
    return [spread(tile[:, first + j : first + j + 1]) for j in range(STEP)]


def row_of(tile, i):
    return spread(tile[i : i + 1, :])


def tree_sum(terms):
    while len(terms) > 1:
        terms = [terms[i] + terms[i + 1] for i in range(0, len(terms), 2)]
    return terms[0]


def factor_half(mat):
    lane = lax.broadcasted_iota(jnp.int32, (STEP, HALF), 1)
    row = lax.broadcasted_iota(jnp.int32, (STEP, HALF), 0)
    count = HALF // STEP
    tiles = [mat[STEP * t : STEP * t + STEP, :] for t in range(count)]
    pivot_cols = lane_columns(tiles[0], 0)
    cols = {t: lane_columns(tiles[t], 0) for t in range(1, count)}
    ahead = lane_columns(tiles[1], STEP)
    done = []
    for h in range(count):
        k = STEP * h
        last = h == count - 1
        inside = (lane >= k) & (lane < k + STEP)
        p = {(i, j): row_of(pivot_cols[i], j) for i in range(STEP) for j in range(i, STEP)}
        u = [jnp.where(inside, jnp.where(lane == k + i, 1.0, 0.0), row_of(tiles[h], i)) for i in range(STEP)]
        low, inv, root = {}, [None] * STEP, [None] * STEP
        for i in range(STEP):
            root[i] = lax.rsqrt(p[i, i])
            inv[i] = root[i] * root[i]
            for j in range(i + 1, STEP):
                low[j, i] = p[i, j] * inv[i]
            for j in range(i + 1, STEP):
                for m in range(j, STEP):
                    p[j, m] = p[j, m] - low[j, i] * p[i, m]
            for j in range(i + 1, STEP):
                u[j] = u[j] - low[j, i] * u[i]
                if not last:
                    cols[h + 1][j] = cols[h + 1][j] - low[j, i] * cols[h + 1][i]
        final = u[0] * root[0]
        for i in range(1, STEP):
            final = jnp.where(row == i, u[i] * root[i], final)
        done.append(jnp.where(lane <= row + k, final, 0.0))
        if last:
            break
        scaled = [cols[h + 1][m] * inv[m] for m in range(STEP)]
        pivot_cols = [
            ahead[j] - tree_sum([scaled[m] * row_of(cols[h + 1][m], j) for m in range(STEP)])
            for j in range(STEP)
        ]
        v = [u[i] * inv[i] for i in range(STEP)]
        for t in range(h + 1, count):
            if t > h + 1:
                for i in range(STEP):
                    for j in range(i + 1, STEP):
                        cols[t][j] = cols[t][j] - low[j, i] * cols[t][i]
            update = tree_sum([cols[t][j] * v[j] for j in range(STEP)])
            tiles[t] = jnp.where(inside, 0.0, tiles[t]) - update
            if t > h + 1:
                cols[t] = lane_columns(tiles[t], k + STEP)
            if t == h + 2:
                ahead = lane_columns(tiles[t], k + 2 * STEP)
    return jnp.concatenate(done, axis=0)


def solve_kernel(corr_ref, rhs_ref, out_ref, aug, diag, first_inv, coupling):
    channels = corr_ref.shape[1]
    order = LAGS * channels
    block = 2 * HALF
    count = order // block
    local = rhs_ref.shape[1]
    total = order + local

    value = corr_ref[0]
    same = lax.broadcasted_iota(jnp.int32, value.shape, 0) == lax.broadcasted_iota(jnp.int32, value.shape, 1)
    trace = jnp.sum(jnp.where(same, value, 0.0))
    value = value + jnp.where(same, 0.1 * (trace / channels) + 1e-06, 0.0)
    for lag in range(LAGS):
        for low in range(LAGS - lag):
            rows, cols = (low + lag) * channels, low * channels
            aug[rows : rows + channels, cols : cols + channels] = value if lag == 0 else corr_ref[lag]
    for tap in range(LAGS):
        aug[order:, tap * channels : (tap + 1) * channels] = rhs_ref[tap]
    diag[...] = value[:HALF, :HALF]

    def step(half_step, carry):
        diag[...] = factor_half(diag[...])
        for b in range(count):
            o = b * block
            mid, end = o + HALF, o + block

            @pl.when(half_step == 2 * b)
            def _():
                low = mm(aug[mid:end, o:mid], diag[...], ((1,), (1,)))
                first_inv[...] = diag[...]
                coupling[...] = low
                diag[...] = aug[mid:end, mid:end] - mm(low, low, ((1,), (1,)))

            @pl.when(half_step == 2 * b + 1)
            def _():
                top, last = first_inv[...], diag[...]
                aug[o:mid, o:mid] = top
                aug[o:mid, mid:end] = jnp.zeros((HALF, HALF), jnp.float32)
                aug[mid:end, o:mid] = -mm(last, mm(coupling[...], top))
                aug[mid:end, mid:end] = last
                aug[end:, o:end] = mm(aug[end:, o:end], aug[o:end, o:end], ((1,), (1,)))
                for c in range(end, order, block):
                    aug[c:, c : c + block] = aug[c:, c : c + block] - mm(
                        aug[c:, o:end], aug[c : c + block, o:end], ((1,), (1,))
                    )
                if end < order:
                    diag[...] = aug[end : end + HALF, end : end + HALF]

        return carry

    lax.fori_loop(0, 2 * count, step, 0)
    for b in range(count - 1, -1, -1):
        o, end = b * block, (b + 1) * block
        known = aug[order:, o:end]
        if end < order:
            known = known - mm(aug[order:, end:order], aug[end:order, o:end])
        aug[order:, o:end] = mm(known, aug[o:end, o:end])
    out_ref[...] = aug[order:, :].astype(jnp.bfloat16)


def solve(corr, rhs):
    channels = corr.shape[1]
    local = rhs.shape[1]
    order = LAGS * channels
    vm = pl.BlockSpec(memory_space=pltpu.VMEM)
    return pl.pallas_call(
        solve_kernel,
        out_shape=jax.ShapeDtypeStruct((local, order), jnp.bfloat16),
        in_specs=[vm, vm],
        out_specs=vm,
        scratch_shapes=[
            pltpu.VMEM((order + local, order), jnp.float32),
            pltpu.VMEM((HALF, HALF), jnp.float32),
            pltpu.VMEM((HALF, HALF), jnp.float32),
            pltpu.VMEM((HALF, HALF), jnp.float32),
        ],
        compiler_params=pltpu.CompilerParams(vmem_limit_bytes=40 << 20),
        name="block_solve",
    )(corr, rhs)


MESH = pl.DeviceIdType.MESH
FINE = 128


def dft_table(samples, band_size):
    times = np.arange(samples, dtype=np.int64)
    harmonic = np.arange(1, band_size + 1, dtype=np.int64)
    phase = (times[:, None] * harmonic[None, :]) % (2 * samples)
    circle = np.arange(2 * samples).astype(np.float32) * np.float32(np.pi / samples)
    cosines = np.cos(circle.astype(np.float64)).astype(np.float32).astype(ml_dtypes.bfloat16)[phase]
    sines = np.sin(circle.astype(np.float64)).astype(np.float32).astype(ml_dtypes.bfloat16)[phase]
    pair = np.stack([cosines.reshape(samples, -1, FINE), sines.reshape(samples, -1, FINE)], axis=2)
    return pair.reshape(samples, 2 * band_size)


def low_bit(value):
    return value & -value


def front_kernel(
    shape, scales, x_hbm, table_hbm, live_ref, cos_ref, sin_ref, all_ref, sys_ref, rhs_ref,
    x_v, tab_v, rot_v, acc_v, part_v, recv_v, full_v, rfull_v,
    x_sem, tab_sem, spec_send, spec_recv, red_send, red_recv, piece_send, piece_recv, lag_send, lag_recv,
):
    shots, shot_shards, lag_shards = shape
    rows, samples = x_v.shape
    local = rows // shots
    chunks = all_ref.shape[0]
    wide = 2 * FINE
    block = samples // x_sem.shape[0]
    my_shot, my_lag = lax.axis_index("shot"), lax.axis_index("lag")
    bits = [1 << i for i in range(lag_shards.bit_length() - 2, -1, -1)]

    def x_copy(b):
        span = pl.ds(b * block, block)
        return pltpu.make_async_copy(x_hbm.at[:, span], x_v.at[:, span], x_sem.at[b])

    def first_copy(b):
        span = pl.ds(b * block, block)
        return pltpu.make_async_copy(
            table_hbm.at[span, pl.ds(0, wide)], tab_v.at[0, span], tab_sem.at[chunks + b]
        )

    def table_copy(c):
        return pltpu.make_async_copy(
            table_hbm.at[:, pl.ds(c * wide, wide)], tab_v.at[c], tab_sem.at[c]
        )

    blocks = x_sem.shape[0]
    for b in range(blocks):
        x_copy(b).start()
        first_copy(b).start()
    for c in range(1, chunks):
        table_copy(c).start()

    barrier = pltpu.get_barrier_semaphore()
    for j in range(1, shot_shards):
        pl.semaphore_signal(barrier, inc=1, device_id=(my_shot ^ j, my_lag), device_id_type=MESH)
    for v in bits:
        pl.semaphore_signal(barrier, inc=1, device_id=(my_shot, my_lag ^ v), device_id_type=MESH)

    def own_rows(lag):
        return pl.ds(pl.multiple_of(lag * local, local), local)

    def spec_copy(c, delta):
        v = low_bit(delta)
        span = own_rows(my_lag ^ (delta ^ v))
        return pltpu.make_async_remote_copy(
            src_ref=all_ref.at[c, span], dst_ref=all_ref.at[c, span],
            send_sem=spec_send.at[c, delta], recv_sem=spec_recv.at[c, delta],
            device_id=(my_shot, my_lag ^ v), device_id_type=MESH,
        )

    def spec_arrival(c, delta):
        v = low_bit(delta)
        span = own_rows(my_lag ^ delta)
        return pltpu.make_async_remote_copy(
            src_ref=all_ref.at[c, span], dst_ref=all_ref.at[c, span],
            send_sem=spec_send.at[c, delta], recv_sem=spec_recv.at[c, delta],
            device_id=(my_shot, my_lag ^ v), device_id_type=MESH,
        )

    def transform(c, loaded):
        total = None
        for b in range(blocks):
            if loaded is not None:
                loaded(b)
            term = jnp.dot(
                x_v[:, b * block : (b + 1) * block], tab_v[c, b * block : (b + 1) * block, :],
                preferred_element_type=jnp.float32,
            )
            total = term if total is None else total + term
        value = (total * live_ref[...]).astype(jnp.bfloat16)
        for s in range(shots):
            all_ref[c, own_rows(my_lag), s * wide : (s + 1) * wide] = value[s * local : (s + 1) * local]

    def send_own(c):
        for v in bits:
            spec_copy(c, v).start()

    def first_loaded(b):
        x_copy(b).wait()
        first_copy(b).wait()

    transform(0, first_loaded)
    pl.semaphore_wait(barrier, shot_shards - 1 + len(bits))
    send_own(0)

    def transform_step(c, carry):
        table_copy(c).wait()
        transform(c, None)
        send_own(c)
        return carry

    lax.fori_loop(1, chunks, transform_step, 0)
    acc_v[...] = jnp.zeros_like(acc_v)
    deltas = sorted(range(1, lag_shards), key=lambda d: -low_bit(d))

    def correlate_step(c, carry):
        for delta in deltas:
            if low_bit(delta) > 1:
                spec_arrival(c, delta).wait_recv()
                for v in bits:
                    if v < low_bit(delta):
                        spec_copy(c, delta | v).start()
        own = all_ref[c, own_rows(my_lag), :].astype(jnp.float32)
        for k in range(2 * LAGS):
            cosine, sine = cos_ref[c, k : k + 1, :], sin_ref[c, k : k + 1, :]
            for s in range(shots):
                o = s * wide
                real, imag = own[:, o : o + FINE], own[:, o + FINE : o + wide]
                rot_v[k * local : (k + 1) * local, o : o + FINE] = (real * cosine - imag * sine).astype(jnp.bfloat16)
                rot_v[k * local : (k + 1) * local, o + FINE : o + wide] = (imag * cosine + real * sine).astype(jnp.bfloat16)
        for delta in deltas:
            if low_bit(delta) == 1:
                spec_arrival(c, delta).wait_recv()
        acc_v[...] = acc_v[...] + lax.dot_general(
            rot_v[...], all_ref[c], (((1,), (1,)), ((), ())), preferred_element_type=jnp.float32
        )
        return carry

    lax.fori_loop(0, chunks, correlate_step, 0)

    half_rows = LAGS * local
    piece = part_v.shape[2]
    for h in range(2):
        for p in range(shot_shards):
            top, lane = h * half_rows + (p // 2) * piece, (p % 2) * FINE
            part_v[h, p] = acc_v[top : top + piece, lane : lane + FINE]

    def reduce_copy(h, j):
        return pltpu.make_async_remote_copy(
            src_ref=part_v.at[h, my_shot ^ j], dst_ref=recv_v.at[h, j],
            send_sem=red_send.at[h, j], recv_sem=red_recv.at[h, j],
            device_id=(my_shot ^ j, my_lag), device_id_type=MESH,
        )

    for h in range(2):
        for j in range(1, shot_shards):
            reduce_copy(h, j).start()

    def piece_copy(h, j, owner):
        ref = full_v.at[my_lag, owner] if h == 0 else rfull_v.at[owner]
        return pltpu.make_async_remote_copy(
            src_ref=ref, dst_ref=ref,
            send_sem=piece_send.at[h, j], recv_sem=piece_recv.at[h, j],
            device_id=(my_shot ^ j, my_lag), device_id_type=MESH,
        )

    def lag_copy(j, delta, arriving):
        v = low_bit(delta)
        ref = full_v.at[my_lag ^ (delta if arriving else delta ^ v), my_shot ^ j]
        return pltpu.make_async_remote_copy(
            src_ref=ref, dst_ref=ref,
            send_sem=lag_send.at[j, delta], recv_sem=lag_recv.at[j, delta],
            device_id=(my_shot, my_lag ^ v), device_id_type=MESH,
        )

    def reduce(h):
        total = part_v[h, my_shot]
        for j in range(1, shot_shards):
            reduce_copy(h, j).wait_recv()
            total = total + recv_v[h, j]
        total = total * scales[0] * scales[1]
        if h == 0:
            full_v[my_lag, my_shot] = total
        else:
            rfull_v[my_shot] = total
        for j in range(1, shot_shards):
            piece_copy(h, j, my_shot).start()

    reduce(0)
    for v in bits:
        lag_copy(0, v, False).start()
    reduce(1)
    for j in range(1, shot_shards):
        piece_copy(0, j, my_shot ^ j).wait_recv()
        for v in bits:
            lag_copy(j, v, False).start()
    for j in range(shot_shards):
        for delta in deltas:
            if low_bit(delta) > 1:
                lag_copy(j, delta, True).wait_recv()
                for v in bits:
                    if v < low_bit(delta):
                        lag_copy(j, delta | v, False).start()
    unit = min(piece, local)
    for j in range(1, shot_shards):
        piece_copy(1, j, my_shot ^ j).wait_recv()
    for p in range(shot_shards):
        for r in range(0, piece, unit):
            row, lane = (p // 2) * piece + r, (p % 2) * FINE
            k, a = row // local, row % local
            rhs_ref[k, a : a + unit, lane : lane + FINE] = rfull_v[p, r : r + unit]
    for j in range(shot_shards):
        for delta in deltas:
            if low_bit(delta) == 1:
                lag_copy(j, delta, True).wait_recv()
    for q in range(lag_shards):
        for p in range(shot_shards):
            for r in range(0, piece, unit):
                row, lane = (p // 2) * piece + r, (p % 2) * FINE
                k, a = row // local, row % local + q * local
                sys_ref[k, a : a + unit, lane : lane + FINE] = full_v[q, p, r : r + unit]
    for c in range(chunks):
        for delta in deltas:
            spec_copy(c, delta).wait_send()
    for h in range(2):
        for j in range(1, shot_shards):
            reduce_copy(h, j).wait_send()
            piece_copy(h, j, my_shot).wait_send()
    for j in range(shot_shards):
        for delta in deltas:
            lag_copy(j, delta, False).wait_send()


def front(traces, table, live, cosine, sine, shot_shards, lag_shards):
    shots, local, samples = traces.shape
    rows = shots * local
    width = table.shape[1]
    chunks = width // (2 * FINE)
    channels = local * lag_shards
    blocks = 4
    piece = 2 * LAGS * local // shot_shards
    total_shots = shots * shot_shards
    scales = (1.0 / samples, 1.0 / (samples * total_shots))
    hbm = pl.BlockSpec(memory_space=pl.ANY)
    vm = pl.BlockSpec(memory_space=pltpu.VMEM)
    sem = pltpu.SemaphoreType.DMA
    return pl.pallas_call(
        functools.partial(front_kernel, (shots, shot_shards, lag_shards), scales),
        out_shape=(
            jax.ShapeDtypeStruct((chunks, channels, shots * 2 * FINE), jnp.bfloat16),
            jax.ShapeDtypeStruct((LAGS, channels, channels), jnp.float32),
            jax.ShapeDtypeStruct((LAGS, local, channels), jnp.float32),
        ),
        in_specs=[hbm, hbm, vm, vm, vm],
        out_specs=(vm, vm, vm),
        scratch_shapes=[
            pltpu.VMEM((rows, samples), jnp.bfloat16),
            pltpu.VMEM((chunks, samples, 2 * FINE), jnp.bfloat16),
            pltpu.VMEM((2 * LAGS * local, shots * 2 * FINE), jnp.bfloat16),
            pltpu.VMEM((2 * LAGS * local, channels), jnp.float32),
            pltpu.VMEM((2, shot_shards, piece, FINE), jnp.float32),
            pltpu.VMEM((2, shot_shards, piece, FINE), jnp.float32),
            pltpu.VMEM((lag_shards, shot_shards, piece, FINE), jnp.float32),
            pltpu.VMEM((shot_shards, piece, FINE), jnp.float32),
            sem((blocks,)),
            sem((chunks + blocks,)),
            sem((chunks, lag_shards)),
            sem((chunks, lag_shards)),
            sem((2, shot_shards)),
            sem((2, shot_shards)),
            sem((2, shot_shards)),
            sem((2, shot_shards)),
            sem((shot_shards, lag_shards)),
            sem((shot_shards, lag_shards)),
        ],
        compiler_params=pltpu.CompilerParams(
            collective_id=0, has_side_effects=True, vmem_limit_bytes=50 << 20
        ),
        name="front",
    )(traces.reshape(rows, samples), table, live, cosine, sine)


def tail_kernel(shots, scale, all_ref, filter_ref, cos_ref, sin_ref, live_ref, table_ref, out_ref, err_v):
    chunks = all_ref.shape[0]
    local = filter_ref.shape[0]
    channels = all_ref.shape[1]
    wide = 2 * FINE
    my_lag = lax.axis_index("lag")

    @pl.when(pl.program_id(0) == 0)
    def _():
        taps = jnp.concatenate(
            [filter_ref[:, j * channels : (j + 1) * channels] for j in range(LAGS)], axis=0
        )

        def chunk_step(c, carry):
            own = all_ref[c, pl.ds(pl.multiple_of(my_lag * local, local), local), :].astype(jnp.float32)
            mixed = jnp.dot(taps, all_ref[c], preferred_element_type=jnp.float32)
            for s in range(shots):
                o = s * wide
                real, imag = own[:, o : o + FINE], own[:, o + FINE : o + wide]
                for j in range(LAGS):
                    cosine, sine = cos_ref[c, LAGS + j : LAGS + j + 1, :], sin_ref[c, LAGS + j : LAGS + j + 1, :]
                    a = mixed[j * local : (j + 1) * local, o : o + FINE]
                    b = mixed[j * local : (j + 1) * local, o + FINE : o + wide]
                    real = real - (a * cosine - b * sine)
                    imag = imag - (b * cosine + a * sine)
                err_v[c, s * local : (s + 1) * local, :FINE] = real.astype(jnp.bfloat16)
                err_v[c, s * local : (s + 1) * local, FINE:] = imag.astype(jnp.bfloat16)
            return carry

        lax.fori_loop(0, chunks, chunk_step, 0)

    error = jnp.concatenate([err_v[c] for c in range(chunks)], axis=1)
    value = lax.dot_general(
        error, table_ref[...], (((1,), (1,)), ((), ())), preferred_element_type=jnp.float32
    )
    out_ref[...] = (value * scale * live_ref[...]).astype(jnp.bfloat16)


def tail(all_spec, filter_rows, cosine, sine, live, table, shots):
    samples, depth = table.shape
    rows = live.shape[0]
    step = min(1024, samples)

    def whole(array):
        return pl.BlockSpec(array.shape, lambda t: (0,) * array.ndim)

    return pl.pallas_call(
        functools.partial(tail_kernel, shots, 1.0 / samples),
        out_shape=jax.ShapeDtypeStruct((rows, samples), jnp.bfloat16),
        grid=(samples // step,),
        in_specs=[
            whole(all_spec), whole(filter_rows), whole(cosine), whole(sine), whole(live),
            pl.BlockSpec((step, depth), lambda t: (t, 0)),
        ],
        out_specs=pl.BlockSpec((rows, step), lambda t: (0, t)),
        scratch_shapes=[pltpu.VMEM((depth // (2 * FINE), rows, 2 * FINE), jnp.bfloat16)],
        compiler_params=pltpu.CompilerParams(vmem_limit_bytes=40 << 20),
        name="tail",
    )(all_spec, filter_rows, cosine, sine, live, table)


def delay_tables(delays, samples, band_size):
    harmonic = jnp.arange(1, band_size + 1, dtype=jnp.int32)
    phase = delays[:, None] * harmonic[None, :] % (2 * samples)
    angle = phase.astype(jnp.float32) * (jnp.pi / samples)
    return (jnp.cos(angle), jnp.sin(angle))


def shards(traces, live_mask, gap_samples):
    shot_count, local_chan, samples = traces.shape
    band_size = samples // 16
    shot_shards, lag_shards = lax.axis_size("shot"), lax.axis_size("lag")
    table = jnp.asarray(dft_table(samples, band_size))
    rows = shot_count * local_chan
    live = live_mask.astype(jnp.float32).reshape(rows, 1)
    spacing = samples // (2 * band_size)
    tap_delays = jnp.arange(LAGS, dtype=jnp.int32) * spacing
    lag_list = jnp.concatenate([tap_delays, gap_samples[0] + tap_delays])
    cosine, sine = delay_tables(lag_list, samples, band_size)

    def by_chunk(x):
        return x.reshape(2 * LAGS, band_size // FINE, FINE).transpose(1, 0, 2)

    cosine, sine = by_chunk(cosine), by_chunk(sine)
    turn = jnp.where(jnp.arange(2 * LAGS) < LAGS, 1.0, -1.0)[None, :, None]
    all_spec, system, rhs = front(traces, table, live, cosine, sine * turn, shot_shards, lag_shards)
    filter_rows = solve(system, rhs)
    restored = tail(all_spec, filter_rows, cosine, sine, live, table, shot_count)
    return restored.reshape(shot_count, local_chan, samples)


def solution(mesh):
    placed = (P("shot", "lag", None), P("shot", "lag"), P())
    return jax.shard_map(
        shards, mesh=mesh, in_specs=placed, out_specs=P("shot", "lag", None), check_vma=False
    )
```

```python
import functools

import jax
import jax.numpy as jnp
import ml_dtypes
import numpy as np
from jax import lax
from jax.experimental import pallas as pl
from jax.experimental.pallas import tpu as pltpu
from jax.sharding import PartitionSpec as P

LAGS=4
HALF=128
STEP=8

def mm(a, b, dims=((1,), (0,))):
    return lax.dot_general(a, b, (dims, ((), ())), precision=lax.Precision.HIGHEST, preferred_element_type=jnp.float32)


def spread(x):
    return jnp.broadcast_to(x, (STEP, HALF))


def lane_columns(tile, first):
    return [spread(tile[:, first + j : first + j + 1]) for j in range(STEP)]


def row_of(tile, i):
    return spread(tile[i : i + 1, :])


def tree_sum(terms):
    while len(terms) > 1:
        terms = [terms[i] + terms[i + 1] for i in range(0, len(terms), 2)]
    return terms[0]


def factor_half(mat):
    lane = lax.broadcasted_iota(jnp.int32, (STEP, HALF), 1)
    row = lax.broadcasted_iota(jnp.int32, (STEP, HALF), 0)
    count = HALF // STEP
    tiles = [mat[STEP * t : STEP * t + STEP, :] for t in range(count)]
    pivot_cols = lane_columns(tiles[0], 0)
    cols = {t: lane_columns(tiles[t], 0) for t in range(1, count)}
    ahead = lane_columns(tiles[1], STEP)
    done = []
    for h in range(count):
        k = STEP * h
        last = h == count - 1
        inside = (lane >= k) & (lane < k + STEP)
        p = {(i, j): row_of(pivot_cols[i], j) for i in range(STEP) for j in range(i, STEP)}
        u = [jnp.where(inside, jnp.where(lane == k + i, 1.0, 0.0), row_of(tiles[h], i)) for i in range(STEP)]
        low, inv, root = {}, [None] * STEP, [None] * STEP
        for i in range(STEP):
            root[i] = lax.rsqrt(p[i, i])
            inv[i] = root[i] * root[i]
            for j in range(i + 1, STEP):
                low[j, i] = p[i, j] * inv[i]
            for j in range(i + 1, STEP):
                for m in range(j, STEP):
                    p[j, m] = p[j, m] - low[j, i] * p[i, m]
            for j in range(i + 1, STEP):
                u[j] = u[j] - low[j, i] * u[i]
                if not last:
                    cols[h + 1][j] = cols[h + 1][j] - low[j, i] * cols[h + 1][i]
        final = u[0] * root[0]
        for i in range(1, STEP):
            final = jnp.where(row == i, u[i] * root[i], final)
        done.append(jnp.where(lane <= row + k, final, 0.0))
        if last:
            break
        scaled = [cols[h + 1][m] * inv[m] for m in range(STEP)]
        pivot_cols = [
            ahead[j] - tree_sum([scaled[m] * row_of(cols[h + 1][m], j) for m in range(STEP)])
            for j in range(STEP)
        ]
        v = [u[i] * inv[i] for i in range(STEP)]
        for t in range(h + 1, count):
            if t > h + 1:
                for i in range(STEP):
                    for j in range(i + 1, STEP):
                        cols[t][j] = cols[t][j] - low[j, i] * cols[t][i]
            update = tree_sum([cols[t][j] * v[j] for j in range(STEP)])
            tiles[t] = jnp.where(inside, 0.0, tiles[t]) - update
            if t > h + 1:
                cols[t] = lane_columns(tiles[t], k + STEP)
            if t == h + 2:
                ahead = lane_columns(tiles[t], k + 2 * STEP)
    return jnp.concatenate(done, axis=0)


def solve_kernel(corr_ref, rhs_ref, out_ref, aug, diag, first_inv, coupling):
    channels = corr_ref.shape[1]
    order = LAGS * channels
    block = 2 * HALF
    count = order // block
    local = rhs_ref.shape[1]
    total = order + local

    value = corr_ref[0]
    same = lax.broadcasted_iota(jnp.int32, value.shape, 0) == lax.broadcasted_iota(jnp.int32, value.shape, 1)
    trace = jnp.sum(jnp.where(same, value, 0.0))
    value = value + jnp.where(same, 0.1 * (trace / channels) + 1e-06, 0.0)
    for lag in range(LAGS):
        for low in range(LAGS - lag):
            rows, cols = (low + lag) * channels, low * channels
            aug[rows : rows + channels, cols : cols + channels] = value if lag == 0 else corr_ref[lag]
    for tap in range(LAGS):
        aug[order:, tap * channels : (tap + 1) * channels] = rhs_ref[tap]
    diag[...] = value[:HALF, :HALF]

    def step(half_step, carry):
        diag[...] = factor_half(diag[...])
        for b in range(count):
            o = b * block
            mid, end = o + HALF, o + block

            @pl.when(half_step == 2 * b)
            def _():
                low = mm(aug[mid:end, o:mid], diag[...], ((1,), (1,)))
                first_inv[...] = diag[...]
                coupling[...] = low
                diag[...] = aug[mid:end, mid:end] - mm(low, low, ((1,), (1,)))

            @pl.when(half_step == 2 * b + 1)
            def _():
                top, last = first_inv[...], diag[...]
                aug[o:mid, o:mid] = top
                aug[o:mid, mid:end] = jnp.zeros((HALF, HALF), jnp.float32)
                aug[mid:end, o:mid] = -mm(last, mm(coupling[...], top))
                aug[mid:end, mid:end] = last
                aug[end:, o:end] = mm(aug[end:, o:end], aug[o:end, o:end], ((1,), (1,)))
                for c in range(end, order, block):
                    aug[c:, c : c + block] = aug[c:, c : c + block] - mm(
                        aug[c:, o:end], aug[c : c + block, o:end], ((1,), (1,))
                    )
                if end < order:
                    diag[...] = aug[end : end + HALF, end : end + HALF]

        return carry

    lax.fori_loop(0, 2 * count, step, 0)
    for b in range(count - 1, -1, -1):
        o, end = b * block, (b + 1) * block
        known = aug[order:, o:end]
        if end < order:
            known = known - mm(aug[order:, end:order], aug[end:order, o:end])
        aug[order:, o:end] = mm(known, aug[o:end, o:end])
    out_ref[...] = aug[order:, :].astype(jnp.bfloat16)


def solve(corr, rhs):
    channels = corr.shape[1]
    local = rhs.shape[1]
    order = LAGS * channels
    vm = pl.BlockSpec(memory_space=pltpu.VMEM)
    return pl.pallas_call(
        solve_kernel,
        out_shape=jax.ShapeDtypeStruct((local, order), jnp.bfloat16),
        in_specs=[vm, vm],
        out_specs=vm,
        scratch_shapes=[
            pltpu.VMEM((order + local, order), jnp.float32),
            pltpu.VMEM((HALF, HALF), jnp.float32),
            pltpu.VMEM((HALF, HALF), jnp.float32),
            pltpu.VMEM((HALF, HALF), jnp.float32),
        ],
        compiler_params=pltpu.CompilerParams(vmem_limit_bytes=40 << 20),
        name="block_solve",
    )(corr, rhs)


MESH = pl.DeviceIdType.MESH
FINE = 128


def dft_table(samples, band_size):
    times = np.arange(samples, dtype=np.int64)
    harmonic = np.arange(1, band_size + 1, dtype=np.int64)
    phase = (times[:, None] * harmonic[None, :]) % (2 * samples)
    circle = np.arange(2 * samples).astype(np.float32) * np.float32(np.pi / samples)
    cosines = np.cos(circle.astype(np.float64)).astype(np.float32).astype(ml_dtypes.bfloat16)[phase]
    sines = np.sin(circle.astype(np.float64)).astype(np.float32).astype(ml_dtypes.bfloat16)[phase]
    pair = np.stack([cosines.reshape(samples, -1, FINE), sines.reshape(samples, -1, FINE)], axis=2)
    return pair.reshape(samples, 2 * band_size)


def low_bit(value):
    return value & -value


def front_kernel(
    shape, scales, x_hbm, table_hbm, live_ref, cos_ref, sin_ref, spec_ref, sys_ref, rhs_ref,
    x_v, tab_v, all_v, rot_v, acc_v, part_v, recv_v, full_v, rfull_v,
    x_sem, tab_sem, out_sem, spec_send, spec_recv, red_send, red_recv, piece_send, piece_recv, lag_send, lag_recv,
):
    shots, shot_shards, lag_shards = shape
    rows, samples = x_v.shape
    local = rows // shots
    chunks = all_v.shape[0]
    channels = all_v.shape[1]
    wide = 2 * FINE
    blocks = x_sem.shape[0]
    block = samples // blocks
    my_shot, my_lag = lax.axis_index("shot"), lax.axis_index("lag")
    bits = [1 << i for i in range(lag_shards.bit_length() - 2, -1, -1)]
    deltas = sorted(range(1, lag_shards), key=lambda d: -low_bit(d))
    near = [d for d in deltas if d < lag_shards // 2]
    far = [d for d in deltas if d >= lag_shards // 2]
    half = channels // 2
    my_half = my_lag // (lag_shards // 2)

    def x_copy(b):
        span = pl.ds(b * block, block)
        return pltpu.make_async_copy(x_hbm.at[:, span], x_v.at[:, span], x_sem.at[b])

    def first_copy(b):
        span = pl.ds(b * block, block)
        return pltpu.make_async_copy(
            table_hbm.at[span, pl.ds(0, wide)], tab_v.at[0, span], tab_sem.at[chunks + b]
        )

    def table_copy(c):
        return pltpu.make_async_copy(
            table_hbm.at[:, pl.ds(pl.multiple_of(c * wide, wide), wide)], tab_v.at[c], tab_sem.at[c]
        )

    for b in range(blocks):
        x_copy(b).start()
        first_copy(b).start()

    barrier = pltpu.get_barrier_semaphore()
    for j in range(1, shot_shards):
        pl.semaphore_signal(barrier, inc=1, device_id=(my_shot ^ j, my_lag), device_id_type=MESH)
    for v in bits:
        pl.semaphore_signal(barrier, inc=1, device_id=(my_shot, my_lag ^ v), device_id_type=MESH)

    def rows_of(lag):
        return pl.ds(pl.multiple_of(lag * local, local), local)

    def spec_copy(c, delta, arriving=False):
        v = low_bit(delta)
        span = rows_of(my_lag ^ (delta if arriving else delta ^ v))
        return pltpu.make_async_remote_copy(
            src_ref=all_v.at[c, span], dst_ref=all_v.at[c, span],
            send_sem=spec_send.at[c, delta], recv_sem=spec_recv.at[c, delta],
            device_id=(my_shot, my_lag ^ v), device_id_type=MESH,
        )

    def forward(c, group):
        for delta in group:
            if low_bit(delta) > 1:
                spec_copy(c, delta, True).wait_recv()
                for v in bits:
                    if v < low_bit(delta):
                        spec_copy(c, delta | v).start()

    def settle(c, group):
        for delta in group:
            if low_bit(delta) == 1:
                spec_copy(c, delta, True).wait_recv()

    def transform(c, loaded):
        total = None
        for b in range(blocks):
            if loaded is not None:
                loaded(b)
            term = jnp.dot(
                x_v[:, b * block : (b + 1) * block], tab_v[c, b * block : (b + 1) * block, :],
                preferred_element_type=jnp.float32,
            )
            total = term if total is None else total + term
        value = (total * live_ref[...]).astype(jnp.bfloat16)
        for s in range(shots):
            all_v[c, rows_of(my_lag), s * wide : (s + 1) * wide] = value[s * local : (s + 1) * local]

    def send_own(c):
        for v in bits:
            spec_copy(c, v).start()

    def rotate(c):
        own = all_v[c, rows_of(my_lag), :].astype(jnp.float32)
        for k in range(2 * LAGS):
            cosine, sine = cos_ref[c, k : k + 1, :], sin_ref[c, k : k + 1, :]
            for s in range(shots):
                o = s * wide
                real, imag = own[:, o : o + FINE], own[:, o + FINE : o + wide]
                rot_v[c, k * local : (k + 1) * local, o : o + FINE] = (real * cosine - imag * sine).astype(jnp.bfloat16)
                rot_v[c, k * local : (k + 1) * local, o + FINE : o + wide] = (imag * cosine + real * sine).astype(jnp.bfloat16)

    def correlate(c, h, side):
        acc_v[h] = acc_v[h] + lax.dot_general(
            rot_v[c], all_v[c, pl.ds(pl.multiple_of(side * half, half), half), :],
            (((1,), (1,)), ((), ())), preferred_element_type=jnp.float32,
        )

    def first_loaded(b):
        x_copy(b).wait()
        first_copy(b).wait()
        if b + 1 == blocks:
            for c in range(1, chunks):
                table_copy(c).start()

    acc_v[...] = jnp.zeros_like(acc_v)
    transform(0, first_loaded)
    pl.semaphore_wait(barrier, shot_shards - 1 + len(bits))
    send_own(0)

    def transform_step(c, carry):
        table_copy(c).wait()
        rotate(c - 1)
        transform(c, None)
        send_own(c)
        return carry

    lax.fori_loop(1, chunks, transform_step, 0)
    rotate(chunks - 1)

    def near_step(c, carry):
        forward(c, near)
        settle(c, near)
        correlate(c, 0, my_half)
        return carry

    lax.fori_loop(0, chunks, near_step, 0)

    piece = part_v.shape[2]

    def reduce_copy(e, j):
        return pltpu.make_async_remote_copy(
            src_ref=part_v.at[e, my_shot ^ j], dst_ref=recv_v.at[e, j],
            send_sem=red_send.at[e, j], recv_sem=red_recv.at[e, j],
            device_id=(my_shot ^ j, my_lag), device_id_type=MESH,
        )

    def scatter(h):
        for g in range(2):
            for p in range(shot_shards):
                top = g * LAGS * local + p * piece
                part_v[2 * g + h, p] = acc_v[h, top : top + piece, :]
        for g in range(2):
            for j in range(1, shot_shards):
                reduce_copy(2 * g + h, j).start()

    def piece_copy(e, j, owner):
        ref = full_v.at[my_lag, e, owner] if e < 2 else rfull_v.at[e - 2, owner]
        return pltpu.make_async_remote_copy(
            src_ref=ref, dst_ref=ref,
            send_sem=piece_send.at[e, j], recv_sem=piece_recv.at[e, j],
            device_id=(my_shot ^ j, my_lag), device_id_type=MESH,
        )

    def lag_copy(e, j, delta, arriving=False):
        v = low_bit(delta)
        ref = full_v.at[my_lag ^ (delta if arriving else delta ^ v), e, my_shot ^ j]
        return pltpu.make_async_remote_copy(
            src_ref=ref, dst_ref=ref,
            send_sem=lag_send.at[e, j, delta], recv_sem=lag_recv.at[e, j, delta],
            device_id=(my_shot, my_lag ^ v), device_id_type=MESH,
        )

    def reduce(e):
        total = part_v[e, my_shot]
        for j in range(1, shot_shards):
            reduce_copy(e, j).wait_recv()
            total = total + recv_v[e, j]
        total = total * scales[0] * scales[1]
        if e < 2:
            full_v[my_lag, e, my_shot] = total
        else:
            rfull_v[e - 2, my_shot] = total
        for j in range(1, shot_shards):
            piece_copy(e, j, my_shot).start()

    def share(e):
        for j in range(shot_shards):
            if j:
                piece_copy(e, j, my_shot ^ j).wait_recv()
            for v in bits:
                lag_copy(e, j, v).start()

    def relay(e):
        for j in range(shot_shards):
            for delta in deltas:
                if low_bit(delta) > 1:
                    lag_copy(e, j, delta, True).wait_recv()
                    for v in bits:
                        if v < low_bit(delta):
                            lag_copy(e, j, delta | v).start()

    def far_step(c, carry):
        forward(c, far)
        settle(c, far)
        correlate(c, 1, 1 - my_half)
        return carry

    def out_copy(c):
        return pltpu.make_async_copy(all_v.at[c], spec_ref.at[c], out_sem.at[c])

    scatter(0)
    lax.fori_loop(0, chunks - 1, far_step, 0)
    reduce(0)
    far_step(chunks - 1, 0)
    scatter(1)
    for c in range(chunks):
        out_copy(c).start()
    share(0)
    reduce(2)
    reduce(1)
    reduce(3)
    share(1)
    relay(0)
    relay(1)
    for e in (2, 3):
        for j in range(1, shot_shards):
            piece_copy(e, j, my_shot ^ j).wait_recv()
    unit = min(piece, local)
    for h in range(2):
        side = my_half if h == 0 else 1 - my_half
        lanes = pl.ds(pl.multiple_of(side * half, half), half)
        for p in range(shot_shards):
            for r in range(0, piece, unit):
                k, a = (p * piece + r) // local, (p * piece + r) % local
                rhs_ref[k, a : a + unit, lanes] = rfull_v[h, p, r : r + unit]
    for e in range(2):
        for j in range(shot_shards):
            for delta in deltas:
                if low_bit(delta) == 1:
                    lag_copy(e, j, delta, True).wait_recv()
    for q in range(lag_shards):
        for h in range(2):
            lane = ((q // (lag_shards // 2)) ^ h) * half
            for p in range(shot_shards):
                for r in range(0, piece, unit):
                    k, a = (p * piece + r) // local, (p * piece + r) % local + q * local
                    sys_ref[k, a : a + unit, lane : lane + half] = full_v[q, h, p, r : r + unit]
    for c in range(chunks):
        out_copy(c).wait()
        for delta in deltas:
            spec_copy(c, delta).wait_send()
    for e in range(4):
        for j in range(1, shot_shards):
            reduce_copy(e, j).wait_send()
            piece_copy(e, j, my_shot).wait_send()
    for e in range(2):
        for j in range(shot_shards):
            for delta in deltas:
                lag_copy(e, j, delta).wait_send()


def front(traces, table, live, cosine, sine, shot_shards, lag_shards):
    shots, local, samples = traces.shape
    rows = shots * local
    width = table.shape[1]
    chunks = width // (2 * FINE)
    channels = local * lag_shards
    half = channels // 2
    blocks = 4
    piece = LAGS * local // shot_shards
    total_shots = shots * shot_shards
    scales = (1.0 / samples, 1.0 / (samples * total_shots))
    hbm = pl.BlockSpec(memory_space=pl.ANY)
    vm = pl.BlockSpec(memory_space=pltpu.VMEM)
    sem = pltpu.SemaphoreType.DMA
    return pl.pallas_call(
        functools.partial(front_kernel, (shots, shot_shards, lag_shards), scales),
        out_shape=(
            jax.ShapeDtypeStruct((chunks, channels, shots * 2 * FINE), jnp.bfloat16),
            jax.ShapeDtypeStruct((LAGS, channels, channels), jnp.float32),
            jax.ShapeDtypeStruct((LAGS, local, channels), jnp.float32),
        ),
        in_specs=[hbm, hbm, vm, vm, vm],
        out_specs=(hbm, vm, vm),
        scratch_shapes=[
            pltpu.VMEM((rows, samples), jnp.bfloat16),
            pltpu.VMEM((chunks, samples, 2 * FINE), jnp.bfloat16),
            pltpu.VMEM((chunks, channels, shots * 2 * FINE), jnp.bfloat16),
            pltpu.VMEM((chunks, 2 * LAGS * local, shots * 2 * FINE), jnp.bfloat16),
            pltpu.VMEM((2, 2 * LAGS * local, half), jnp.float32),
            pltpu.VMEM((4, shot_shards, piece, half), jnp.float32),
            pltpu.VMEM((4, shot_shards, piece, half), jnp.float32),
            pltpu.VMEM((lag_shards, 2, shot_shards, piece, half), jnp.float32),
            pltpu.VMEM((2, shot_shards, piece, half), jnp.float32),
            sem((blocks,)),
            sem((chunks + blocks,)),
            sem((chunks,)),
            sem((chunks, lag_shards)),
            sem((chunks, lag_shards)),
            sem((4, shot_shards)),
            sem((4, shot_shards)),
            sem((4, shot_shards)),
            sem((4, shot_shards)),
            sem((2, shot_shards, lag_shards)),
            sem((2, shot_shards, lag_shards)),
        ],
        compiler_params=pltpu.CompilerParams(
            collective_id=0, has_side_effects=True, vmem_limit_bytes=56 << 20
        ),
        name="front",
    )(traces.reshape(rows, samples), table, live, cosine, sine)


def tail_kernel(shots, scale, all_ref, filter_ref, cos_ref, sin_ref, live_ref, table_ref, out_ref, err_v):
    chunks = all_ref.shape[0]
    local = filter_ref.shape[0]
    channels = all_ref.shape[1]
    wide = 2 * FINE
    my_lag = lax.axis_index("lag")

    @pl.when(pl.program_id(0) == 0)
    def _():
        taps = jnp.concatenate(
            [filter_ref[:, j * channels : (j + 1) * channels] for j in range(LAGS)], axis=0
        )

        def chunk_step(c, carry):
            own = all_ref[c, pl.ds(pl.multiple_of(my_lag * local, local), local), :].astype(jnp.float32)
            mixed = jnp.dot(taps, all_ref[c], preferred_element_type=jnp.float32)
            for s in range(shots):
                o = s * wide
                real, imag = own[:, o : o + FINE], own[:, o + FINE : o + wide]
                for j in range(LAGS):
                    cosine, sine = cos_ref[c, LAGS + j : LAGS + j + 1, :], sin_ref[c, LAGS + j : LAGS + j + 1, :]
                    a = mixed[j * local : (j + 1) * local, o : o + FINE]
                    b = mixed[j * local : (j + 1) * local, o + FINE : o + wide]
                    real = real - (a * cosine - b * sine)
                    imag = imag - (b * cosine + a * sine)
                err_v[c, s * local : (s + 1) * local, :FINE] = real.astype(jnp.bfloat16)
                err_v[c, s * local : (s + 1) * local, FINE:] = imag.astype(jnp.bfloat16)
            return carry

        lax.fori_loop(0, chunks, chunk_step, 0)

    error = jnp.concatenate([err_v[c] for c in range(chunks)], axis=1)
    value = lax.dot_general(
        error, table_ref[...], (((1,), (1,)), ((), ())), preferred_element_type=jnp.float32
    )
    out_ref[...] = (value * scale * live_ref[...]).astype(jnp.bfloat16)


def tail(all_spec, filter_rows, cosine, sine, live, table, shots):
    samples, depth = table.shape
    rows = live.shape[0]
    step = min(1024, samples)

    def whole(array):
        return pl.BlockSpec(array.shape, lambda t: (0,) * array.ndim)

    return pl.pallas_call(
        functools.partial(tail_kernel, shots, 1.0 / samples),
        out_shape=jax.ShapeDtypeStruct((rows, samples), jnp.bfloat16),
        grid=(samples // step,),
        in_specs=[
            whole(all_spec), whole(filter_rows), whole(cosine), whole(sine), whole(live),
            pl.BlockSpec((step, depth), lambda t: (t, 0)),
        ],
        out_specs=pl.BlockSpec((rows, step), lambda t: (0, t)),
        scratch_shapes=[pltpu.VMEM((depth // (2 * FINE), rows, 2 * FINE), jnp.bfloat16)],
        compiler_params=pltpu.CompilerParams(vmem_limit_bytes=40 << 20),
        name="tail",
    )(all_spec, filter_rows, cosine, sine, live, table)


def delay_tables(delays, samples, band_size):
    harmonic = jnp.arange(1, band_size + 1, dtype=jnp.int32)
    phase = delays[:, None] * harmonic[None, :] % (2 * samples)
    angle = phase.astype(jnp.float32) * (jnp.pi / samples)
    return (jnp.cos(angle), jnp.sin(angle))


def shards(traces, live_mask, gap_samples):
    shot_count, local_chan, samples = traces.shape
    band_size = samples // 16
    shot_shards, lag_shards = lax.axis_size("shot"), lax.axis_size("lag")
    table = jnp.asarray(dft_table(samples, band_size))
    rows = shot_count * local_chan
    live = live_mask.astype(jnp.float32).reshape(rows, 1)
    spacing = samples // (2 * band_size)
    tap_delays = jnp.arange(LAGS, dtype=jnp.int32) * spacing
    lag_list = jnp.concatenate([tap_delays, gap_samples[0] + tap_delays])
    cosine, sine = delay_tables(lag_list, samples, band_size)

    def by_chunk(x):
        return x.reshape(2 * LAGS, band_size // FINE, FINE).transpose(1, 0, 2)

    cosine, sine = by_chunk(cosine), by_chunk(sine)
    turn = jnp.where(jnp.arange(2 * LAGS) < LAGS, 1.0, -1.0)[None, :, None]
    all_spec, system, rhs = front(traces, table, live, cosine, sine * turn, shot_shards, lag_shards)
    filter_rows = solve(system, rhs)
    restored = tail(all_spec, filter_rows, cosine, sine, live, table, shot_count)
    return restored.reshape(shot_count, local_chan, samples)


def solution(mesh):
    placed = (P("shot", "lag", None), P("shot", "lag"), P())
    return jax.shard_map(
        shards, mesh=mesh, in_specs=placed, out_specs=P("shot", "lag", None), check_vma=False
    )
```

```python
import functools

import jax
import jax.numpy as jnp
import ml_dtypes
import numpy as np
from jax import lax
from jax.experimental import pallas as pl
from jax.experimental.pallas import tpu as pltpu
from jax.sharding import PartitionSpec as P

LAGS=4
HALF=128
STEP=8

def mm(a, b, dims=((1,), (0,))):
    return lax.dot_general(a, b, (dims, ((), ())), precision=lax.Precision.HIGHEST, preferred_element_type=jnp.float32)


def spread(x):
    return jnp.broadcast_to(x, (STEP, HALF))


def lane_columns(tile, first):
    return [spread(tile[:, first + j : first + j + 1]) for j in range(STEP)]


def row_of(tile, i):
    return spread(tile[i : i + 1, :])


def tree_sum(terms):
    while len(terms) > 1:
        terms = [terms[i] + terms[i + 1] for i in range(0, len(terms), 2)]
    return terms[0]


def factor_half(mat):
    lane = lax.broadcasted_iota(jnp.int32, (STEP, HALF), 1)
    row = lax.broadcasted_iota(jnp.int32, (STEP, HALF), 0)
    count = HALF // STEP
    tiles = [mat[STEP * t : STEP * t + STEP, :] for t in range(count)]
    pivot_cols = lane_columns(tiles[0], 0)
    cols = {t: lane_columns(tiles[t], 0) for t in range(1, count)}
    ahead = lane_columns(tiles[1], STEP)
    done = []
    for h in range(count):
        k = STEP * h
        last = h == count - 1
        inside = (lane >= k) & (lane < k + STEP)
        p = {(i, j): row_of(pivot_cols[i], j) for i in range(STEP) for j in range(i, STEP)}
        u = [jnp.where(inside, jnp.where(lane == k + i, 1.0, 0.0), row_of(tiles[h], i)) for i in range(STEP)]
        low, inv, root = {}, [None] * STEP, [None] * STEP
        for i in range(STEP):
            root[i] = lax.rsqrt(p[i, i])
            inv[i] = root[i] * root[i]
            for j in range(i + 1, STEP):
                low[j, i] = p[i, j] * inv[i]
            for j in range(i + 1, STEP):
                for m in range(j, STEP):
                    p[j, m] = p[j, m] - low[j, i] * p[i, m]
            for j in range(i + 1, STEP):
                u[j] = u[j] - low[j, i] * u[i]
                if not last:
                    cols[h + 1][j] = cols[h + 1][j] - low[j, i] * cols[h + 1][i]
        final = u[0] * root[0]
        for i in range(1, STEP):
            final = jnp.where(row == i, u[i] * root[i], final)
        done.append(jnp.where(lane <= row + k, final, 0.0))
        if last:
            break
        scaled = [cols[h + 1][m] * inv[m] for m in range(STEP)]
        pivot_cols = [
            ahead[j] - tree_sum([scaled[m] * row_of(cols[h + 1][m], j) for m in range(STEP)])
            for j in range(STEP)
        ]
        v = [u[i] * inv[i] for i in range(STEP)]
        for t in range(h + 1, count):
            if t > h + 1:
                for i in range(STEP):
                    for j in range(i + 1, STEP):
                        cols[t][j] = cols[t][j] - low[j, i] * cols[t][i]
            update = tree_sum([cols[t][j] * v[j] for j in range(STEP)])
            tiles[t] = jnp.where(inside, 0.0, tiles[t]) - update
            if t > h + 1:
                cols[t] = lane_columns(tiles[t], k + STEP)
            if t == h + 2:
                ahead = lane_columns(tiles[t], k + 2 * STEP)
    return jnp.concatenate(done, axis=0)


def solve_kernel(corr_ref, rhs_ref, out_ref, aug, diag, first_inv, coupling):
    channels = corr_ref.shape[1]
    order = LAGS * channels
    block = 2 * HALF
    count = order // block
    local = rhs_ref.shape[1]
    total = order + local

    value = corr_ref[0]
    same = lax.broadcasted_iota(jnp.int32, value.shape, 0) == lax.broadcasted_iota(jnp.int32, value.shape, 1)
    trace = jnp.sum(jnp.where(same, value, 0.0))
    value = value + jnp.where(same, 0.1 * (trace / channels) + 1e-06, 0.0)
    for lag in range(LAGS):
        for low in range(LAGS - lag):
            rows, cols = (low + lag) * channels, low * channels
            aug[rows : rows + channels, cols : cols + channels] = value if lag == 0 else corr_ref[lag]
    for tap in range(LAGS):
        aug[order:, tap * channels : (tap + 1) * channels] = rhs_ref[tap]
    diag[...] = value[:HALF, :HALF]

    def step(half_step, carry):
        diag[...] = factor_half(diag[...])
        for b in range(count):
            o = b * block
            mid, end = o + HALF, o + block

            @pl.when(half_step == 2 * b)
            def _():
                low = mm(aug[mid:end, o:mid], diag[...], ((1,), (1,)))
                first_inv[...] = diag[...]
                coupling[...] = low
                diag[...] = aug[mid:end, mid:end] - mm(low, low, ((1,), (1,)))

            @pl.when(half_step == 2 * b + 1)
            def _():
                top, last = first_inv[...], diag[...]
                aug[o:mid, o:mid] = top
                aug[o:mid, mid:end] = jnp.zeros((HALF, HALF), jnp.float32)
                aug[mid:end, o:mid] = -mm(last, mm(coupling[...], top))
                aug[mid:end, mid:end] = last
                aug[end:, o:end] = mm(aug[end:, o:end], aug[o:end, o:end], ((1,), (1,)))
                for c in range(end, order, block):
                    aug[c:, c : c + block] = aug[c:, c : c + block] - mm(
                        aug[c:, o:end], aug[c : c + block, o:end], ((1,), (1,))
                    )
                if end < order:
                    diag[...] = aug[end : end + HALF, end : end + HALF]

        return carry

    lax.fori_loop(0, 2 * count, step, 0)
    for b in range(count - 1, -1, -1):
        o, end = b * block, (b + 1) * block
        known = aug[order:, o:end]
        if end < order:
            known = known - mm(aug[order:, end:order], aug[end:order, o:end])
        aug[order:, o:end] = mm(known, aug[o:end, o:end])
    out_ref[...] = aug[order:, :].astype(jnp.bfloat16)


def solve(corr, rhs):
    channels = corr.shape[1]
    local = rhs.shape[1]
    order = LAGS * channels
    vm = pl.BlockSpec(memory_space=pltpu.VMEM)
    return pl.pallas_call(
        solve_kernel,
        out_shape=jax.ShapeDtypeStruct((local, order), jnp.bfloat16),
        in_specs=[vm, vm],
        out_specs=vm,
        scratch_shapes=[
            pltpu.VMEM((order + local, order), jnp.float32),
            pltpu.VMEM((HALF, HALF), jnp.float32),
            pltpu.VMEM((HALF, HALF), jnp.float32),
            pltpu.VMEM((HALF, HALF), jnp.float32),
        ],
        compiler_params=pltpu.CompilerParams(vmem_limit_bytes=40 << 20),
        name="block_solve",
    )(corr, rhs)


MESH = pl.DeviceIdType.MESH
FINE = 128


def dft_table(samples, band_size):
    times = np.arange(samples // 2, dtype=np.int64)
    harmonic = np.arange(1, band_size + 1, dtype=np.int64)
    phase = (times[:, None] * harmonic[None, :]) % (2 * samples)
    circle = np.arange(2 * samples).astype(np.float32) * np.float32(np.pi / samples)
    cosines = np.cos(circle.astype(np.float64)).astype(np.float32).astype(ml_dtypes.bfloat16)[phase]
    sines = np.sin(circle.astype(np.float64)).astype(np.float32).astype(ml_dtypes.bfloat16)[phase]
    pair = np.stack([cosines.reshape(samples // 2, -1, FINE), sines.reshape(samples // 2, -1, FINE)], axis=2)
    return pair.reshape(samples // 2, 2 * band_size)


def low_bit(value):
    return value & -value


def quarter_turn(c, shape):
    harmonic = (lax.broadcasted_iota(jnp.int32, shape, 1) + (c * FINE + 1)) & 3
    cosine = jnp.where(harmonic == 0, 1.0, jnp.where(harmonic == 2, -1.0, 0.0))
    sine = jnp.where(harmonic == 1, 1.0, jnp.where(harmonic == 3, -1.0, 0.0))
    return cosine, sine


def front_kernel(
    shape, scales, x_hbm, table_hbm, live_ref, cos_ref, sin_ref, spec_ref, sys_ref, rhs_ref,
    x_v, tab_v, all_v, rot_v, acc_v, part_v, recv_v, full_v, rfull_v,
    x_sem, tab_sem, out_sem, spec_send, spec_recv, red_send, red_recv, piece_send, piece_recv, lag_send, lag_recv,
):
    shots, shot_shards, lag_shards = shape
    rows, samples = x_v.shape[0] // 2, x_v.shape[1]
    local = rows // shots
    chunks = all_v.shape[0]
    channels = all_v.shape[1]
    wide = 2 * FINE
    blocks = x_sem.shape[0]
    block = samples // blocks
    my_shot, my_lag = lax.axis_index("shot"), lax.axis_index("lag")
    bits = [1 << i for i in range(lag_shards.bit_length() - 2, -1, -1)]
    deltas = sorted(range(1, lag_shards), key=lambda d: -low_bit(d))
    near = [d for d in deltas if d < lag_shards // 2]
    far = [d for d in deltas if d >= lag_shards // 2]
    half = channels // 2
    my_half = my_lag // (lag_shards // 2)

    def x_copy(b, side):
        span = pl.ds(b * block, block)
        return pltpu.make_async_copy(
            x_hbm.at[:, pl.ds(side * samples + b * block, block)],
            x_v.at[pl.ds(side * rows, rows), span], x_sem.at[b, side],
        )

    def first_copy(b):
        span = pl.ds(b * block, block)
        return pltpu.make_async_copy(
            table_hbm.at[span, pl.ds(0, wide)], tab_v.at[0, span], tab_sem.at[chunks + b]
        )

    def table_copy(c):
        return pltpu.make_async_copy(
            table_hbm.at[:, pl.ds(pl.multiple_of(c * wide, wide), wide)], tab_v.at[c], tab_sem.at[c]
        )

    for b in range(blocks):
        first_copy(b).start()
        for side in range(2):
            x_copy(b, side).start()

    barrier = pltpu.get_barrier_semaphore()
    for j in range(1, shot_shards):
        pl.semaphore_signal(barrier, inc=1, device_id=(my_shot ^ j, my_lag), device_id_type=MESH)
    for v in bits:
        pl.semaphore_signal(barrier, inc=1, device_id=(my_shot, my_lag ^ v), device_id_type=MESH)

    def rows_of(lag):
        return pl.ds(pl.multiple_of(lag * local, local), local)

    def spec_copy(c, delta, arriving=False):
        v = low_bit(delta)
        span = rows_of(my_lag ^ (delta if arriving else delta ^ v))
        return pltpu.make_async_remote_copy(
            src_ref=all_v.at[c, span], dst_ref=all_v.at[c, span],
            send_sem=spec_send.at[c, delta], recv_sem=spec_recv.at[c, delta],
            device_id=(my_shot, my_lag ^ v), device_id_type=MESH,
        )

    def forward(c, group):
        for delta in group:
            if low_bit(delta) > 1:
                spec_copy(c, delta, True).wait_recv()
                for v in bits:
                    if v < low_bit(delta):
                        spec_copy(c, delta | v).start()

    def settle(c, group):
        for delta in group:
            if low_bit(delta) == 1:
                spec_copy(c, delta, True).wait_recv()

    def transform(c, loaded):
        total = None
        for b in range(blocks):
            if loaded is not None:
                loaded(b)
            term = jnp.dot(
                x_v[:, b * block : (b + 1) * block], tab_v[c, b * block : (b + 1) * block, :],
                preferred_element_type=jnp.float32,
            )
            total = term if total is None else total + term
        turn_cos, turn_sin = quarter_turn(c, (1, FINE))
        early, late = total[:rows], total[rows:]
        live = live_ref[...]
        real = (early[:, :FINE] + (late[:, :FINE] * turn_cos - late[:, FINE:] * turn_sin)) * live
        imag = (early[:, FINE:] + (late[:, FINE:] * turn_cos + late[:, :FINE] * turn_sin)) * live
        for s in range(shots):
            span, o = slice(s * local, (s + 1) * local), s * wide
            all_v[c, rows_of(my_lag), o : o + FINE] = real[span].astype(jnp.bfloat16)
            all_v[c, rows_of(my_lag), o + FINE : o + wide] = imag[span].astype(jnp.bfloat16)

    def send_own(c):
        for v in bits:
            spec_copy(c, v).start()

    def rotate(c):
        own = all_v[c, rows_of(my_lag), :].astype(jnp.float32)
        for k in range(2 * LAGS):
            cosine, sine = cos_ref[c, k : k + 1, :], sin_ref[c, k : k + 1, :]
            for s in range(shots):
                o = s * wide
                real, imag = own[:, o : o + FINE], own[:, o + FINE : o + wide]
                rot_v[c, k * local : (k + 1) * local, o : o + FINE] = (real * cosine - imag * sine).astype(jnp.bfloat16)
                rot_v[c, k * local : (k + 1) * local, o + FINE : o + wide] = (imag * cosine + real * sine).astype(jnp.bfloat16)

    def correlate(c, h, side):
        acc_v[h] = acc_v[h] + lax.dot_general(
            rot_v[c], all_v[c, pl.ds(pl.multiple_of(side * half, half), half), :],
            (((1,), (1,)), ((), ())), preferred_element_type=jnp.float32,
        )

    def first_loaded(b):
        first_copy(b).wait()
        for side in range(2):
            x_copy(b, side).wait()
        if b + 1 == blocks:
            for c in range(1, chunks):
                table_copy(c).start()

    acc_v[...] = jnp.zeros_like(acc_v)
    transform(0, first_loaded)
    pl.semaphore_wait(barrier, shot_shards - 1 + len(bits))
    send_own(0)

    def transform_step(c, carry):
        table_copy(c).wait()
        rotate(c - 1)
        transform(c, None)
        send_own(c)
        return carry

    lax.fori_loop(1, chunks, transform_step, 0)
    rotate(chunks - 1)

    def near_step(c, carry):
        forward(c, near)
        settle(c, near)
        correlate(c, 0, my_half)
        return carry

    lax.fori_loop(0, chunks, near_step, 0)

    piece = part_v.shape[2]

    def reduce_copy(e, j):
        return pltpu.make_async_remote_copy(
            src_ref=part_v.at[e, my_shot ^ j], dst_ref=recv_v.at[e, j],
            send_sem=red_send.at[e, j], recv_sem=red_recv.at[e, j],
            device_id=(my_shot ^ j, my_lag), device_id_type=MESH,
        )

    def scatter(h):
        for g in range(2):
            for p in range(shot_shards):
                top = g * LAGS * local + p * piece
                part_v[2 * g + h, p] = acc_v[h, top : top + piece, :]
        for g in range(2):
            for j in range(1, shot_shards):
                reduce_copy(2 * g + h, j).start()

    def piece_copy(e, j, owner):
        ref = full_v.at[my_lag, e, owner] if e < 2 else rfull_v.at[e - 2, owner]
        return pltpu.make_async_remote_copy(
            src_ref=ref, dst_ref=ref,
            send_sem=piece_send.at[e, j], recv_sem=piece_recv.at[e, j],
            device_id=(my_shot ^ j, my_lag), device_id_type=MESH,
        )

    def lag_copy(e, j, delta, arriving=False):
        v = low_bit(delta)
        ref = full_v.at[my_lag ^ (delta if arriving else delta ^ v), e, my_shot ^ j]
        return pltpu.make_async_remote_copy(
            src_ref=ref, dst_ref=ref,
            send_sem=lag_send.at[e, j, delta], recv_sem=lag_recv.at[e, j, delta],
            device_id=(my_shot, my_lag ^ v), device_id_type=MESH,
        )

    def reduce(e):
        total = part_v[e, my_shot]
        for j in range(1, shot_shards):
            reduce_copy(e, j).wait_recv()
            total = total + recv_v[e, j]
        total = total * scales[0] * scales[1]
        if e < 2:
            full_v[my_lag, e, my_shot] = total
        else:
            rfull_v[e - 2, my_shot] = total
        for j in range(1, shot_shards):
            piece_copy(e, j, my_shot).start()

    def share(e):
        for j in range(shot_shards):
            if j:
                piece_copy(e, j, my_shot ^ j).wait_recv()
            for v in bits:
                lag_copy(e, j, v).start()

    def relay(e):
        for j in range(shot_shards):
            for delta in deltas:
                if low_bit(delta) > 1:
                    lag_copy(e, j, delta, True).wait_recv()
                    for v in bits:
                        if v < low_bit(delta):
                            lag_copy(e, j, delta | v).start()

    def far_step(c, carry):
        forward(c, far)
        settle(c, far)
        correlate(c, 1, 1 - my_half)
        return carry

    def out_copy(c):
        return pltpu.make_async_copy(all_v.at[c], spec_ref.at[c], out_sem.at[c])

    scatter(0)
    lax.fori_loop(0, chunks - 1, far_step, 0)
    reduce(0)
    far_step(chunks - 1, 0)
    scatter(1)
    for c in range(chunks):
        out_copy(c).start()
    share(0)
    reduce(1)
    reduce(2)
    share(1)
    relay(0)
    reduce(3)
    relay(1)
    for e in (2, 3):
        for j in range(1, shot_shards):
            piece_copy(e, j, my_shot ^ j).wait_recv()
    unit = min(piece, local)
    for h in range(2):
        side = my_half if h == 0 else 1 - my_half
        lanes = pl.ds(pl.multiple_of(side * half, half), half)
        for p in range(shot_shards):
            for r in range(0, piece, unit):
                k, a = (p * piece + r) // local, (p * piece + r) % local
                rhs_ref[k, a : a + unit, lanes] = rfull_v[h, p, r : r + unit]
    for e in range(2):
        for j in range(shot_shards):
            for delta in deltas:
                if low_bit(delta) == 1:
                    lag_copy(e, j, delta, True).wait_recv()
    for q in range(lag_shards):
        for h in range(2):
            lane = ((q // (lag_shards // 2)) ^ h) * half
            for p in range(shot_shards):
                for r in range(0, piece, unit):
                    k, a = (p * piece + r) // local, (p * piece + r) % local + q * local
                    sys_ref[k, a : a + unit, lane : lane + half] = full_v[q, h, p, r : r + unit]
    for c in range(chunks):
        out_copy(c).wait()
        for delta in deltas:
            spec_copy(c, delta).wait_send()
    for e in range(4):
        for j in range(1, shot_shards):
            reduce_copy(e, j).wait_send()
            piece_copy(e, j, my_shot).wait_send()
    for e in range(2):
        for j in range(shot_shards):
            for delta in deltas:
                lag_copy(e, j, delta).wait_send()


def front(traces, table, live, cosine, sine, shot_shards, lag_shards):
    shots, local, samples = traces.shape
    rows = shots * local
    width = table.shape[1]
    chunks = width // (2 * FINE)
    channels = local * lag_shards
    half = channels // 2
    blocks = 4
    piece = LAGS * local // shot_shards
    total_shots = shots * shot_shards
    scales = (1.0 / samples, 1.0 / (samples * total_shots))
    hbm = pl.BlockSpec(memory_space=pl.ANY)
    vm = pl.BlockSpec(memory_space=pltpu.VMEM)
    sem = pltpu.SemaphoreType.DMA
    return pl.pallas_call(
        functools.partial(front_kernel, (shots, shot_shards, lag_shards), scales),
        out_shape=(
            jax.ShapeDtypeStruct((chunks, channels, shots * 2 * FINE), jnp.bfloat16),
            jax.ShapeDtypeStruct((LAGS, channels, channels), jnp.float32),
            jax.ShapeDtypeStruct((LAGS, local, channels), jnp.float32),
        ),
        in_specs=[hbm, hbm, vm, vm, vm],
        out_specs=(hbm, vm, vm),
        scratch_shapes=[
            pltpu.VMEM((2 * rows, samples // 2), jnp.bfloat16),
            pltpu.VMEM((chunks, samples // 2, 2 * FINE), jnp.bfloat16),
            pltpu.VMEM((chunks, channels, shots * 2 * FINE), jnp.bfloat16),
            pltpu.VMEM((chunks, 2 * LAGS * local, shots * 2 * FINE), jnp.bfloat16),
            pltpu.VMEM((2, 2 * LAGS * local, half), jnp.float32),
            pltpu.VMEM((4, shot_shards, piece, half), jnp.float32),
            pltpu.VMEM((4, shot_shards, piece, half), jnp.float32),
            pltpu.VMEM((lag_shards, 2, shot_shards, piece, half), jnp.float32),
            pltpu.VMEM((2, shot_shards, piece, half), jnp.float32),
            sem((blocks, 2)),
            sem((chunks + blocks,)),
            sem((chunks,)),
            sem((chunks, lag_shards)),
            sem((chunks, lag_shards)),
            sem((4, shot_shards)),
            sem((4, shot_shards)),
            sem((4, shot_shards)),
            sem((4, shot_shards)),
            sem((2, shot_shards, lag_shards)),
            sem((2, shot_shards, lag_shards)),
        ],
        compiler_params=pltpu.CompilerParams(
            collective_id=0, has_side_effects=True, vmem_limit_bytes=56 << 20
        ),
        name="front",
    )(traces.reshape(rows, samples), table, live, cosine, sine)


def tail_kernel(
    shots, scale, spec_hbm, filter_ref, cos_ref, sin_ref, live_ref, table_hbm, out_hbm,
    spec_v, tab_v, err_v, stage_v, spec_sem, tab_sem, out_sem,
):
    chunks, channels = spec_v.shape[:2]
    local = filter_ref.shape[0]
    rows = shots * local
    wide = 2 * FINE
    steps, step = tab_v.shape[:2]
    my_lag = lax.axis_index("lag")

    def spec_copy(c):
        return pltpu.make_async_copy(spec_hbm.at[c], spec_v.at[c], spec_sem.at[c])

    def table_copy(t):
        span = pl.ds(pl.multiple_of(t * step, step), step)
        return pltpu.make_async_copy(table_hbm.at[span], tab_v.at[t], tab_sem.at[t])

    def out_copy(t, side):
        span = pl.ds(pl.multiple_of((side * steps + t) * step, step), step)
        slot = lax.rem(t, 2)
        return pltpu.make_async_copy(
            stage_v.at[slot, pl.ds(side * rows, rows)], out_hbm.at[:, span], out_sem.at[slot, side]
        )

    for c in range(chunks):
        spec_copy(c).start()
    for t in range(steps):
        table_copy(t).start()
    taps = jnp.concatenate(
        [filter_ref[:, j * channels : (j + 1) * channels] for j in range(LAGS)], axis=0
    )
    for c in range(chunks):
        spec_copy(c).wait()
        own = spec_v[c, pl.ds(pl.multiple_of(my_lag * local, local), local), :].astype(jnp.float32)
        turn_cos, turn_sin = quarter_turn(c, (1, FINE))
        for s in range(shots):
            o = s * wide
            mixed = jnp.dot(taps, spec_v[c, :, o : o + wide], preferred_element_type=jnp.float32)
            real, imag = own[:, o : o + FINE], own[:, o + FINE : o + wide]
            for j in range(LAGS):
                cosine, sine = cos_ref[c, LAGS + j : LAGS + j + 1, :], sin_ref[c, LAGS + j : LAGS + j + 1, :]
                a = mixed[j * local : (j + 1) * local, :FINE]
                b = mixed[j * local : (j + 1) * local, FINE:]
                real = real - (a * cosine - b * sine)
                imag = imag - (b * cosine + a * sine)
            top, lane = s * local, c * wide
            err_v[top : top + local, lane : lane + FINE] = real.astype(jnp.bfloat16)
            err_v[top : top + local, lane + FINE : lane + wide] = imag.astype(jnp.bfloat16)
            top = rows + top
            err_v[top : top + local, lane : lane + FINE] = (real * turn_cos + imag * turn_sin).astype(jnp.bfloat16)
            err_v[top : top + local, lane + FINE : lane + wide] = (imag * turn_cos - real * turn_sin).astype(jnp.bfloat16)
    live = live_ref[...] * scale

    def back_step(t, carry):
        table_copy(t).wait()

        @pl.when(t >= 2)
        def _():
            for side in range(2):
                out_copy(t - 2, side).wait()

        value = lax.dot_general(
            err_v[...], tab_v[t], (((1,), (1,)), ((), ())), preferred_element_type=jnp.float32
        )
        slot = lax.rem(t, 2)
        for side in range(2):
            stage_v[slot, side * rows : (side + 1) * rows, :] = (
                value[side * rows : (side + 1) * rows] * live
            ).astype(jnp.bfloat16)
            out_copy(t, side).start()
        return carry

    lax.fori_loop(0, steps, back_step, 0)
    for t in range(max(steps - 2, 0), steps):
        for side in range(2):
            out_copy(t, side).wait()


def tail(all_spec, filter_rows, cosine, sine, live, table, shots):
    samples, depth = table.shape
    rows = live.shape[0]
    step = min(512, samples)
    hbm = pl.BlockSpec(memory_space=pl.ANY)
    vm = pl.BlockSpec(memory_space=pltpu.VMEM)
    return pl.pallas_call(
        functools.partial(tail_kernel, shots, 0.5 / samples),
        out_shape=jax.ShapeDtypeStruct((rows, 2 * samples), jnp.bfloat16),
        in_specs=[hbm, vm, vm, vm, vm, hbm],
        out_specs=hbm,
        scratch_shapes=[
            pltpu.VMEM(all_spec.shape, jnp.bfloat16),
            pltpu.VMEM((samples // step, step, depth), jnp.bfloat16),
            pltpu.VMEM((2 * rows, depth), jnp.bfloat16),
            pltpu.VMEM((2, 2 * rows, step), jnp.bfloat16),
            pltpu.SemaphoreType.DMA((all_spec.shape[0],)),
            pltpu.SemaphoreType.DMA((samples // step,)),
            pltpu.SemaphoreType.DMA((2, 2)),
        ],
        compiler_params=pltpu.CompilerParams(vmem_limit_bytes=40 << 20),
        name="tail",
    )(all_spec, filter_rows, cosine, sine, live, table)


def delay_tables(delays, samples, band_size):
    harmonic = jnp.arange(1, band_size + 1, dtype=jnp.int32)
    phase = delays[:, None] * harmonic[None, :] % (2 * samples)
    angle = phase.astype(jnp.float32) * (jnp.pi / samples)
    return (jnp.cos(angle), jnp.sin(angle))


def shards(traces, live_mask, gap_samples):
    shot_count, local_chan, samples = traces.shape
    band_size = samples // 16
    shot_shards, lag_shards = lax.axis_size("shot"), lax.axis_size("lag")
    table = jnp.asarray(dft_table(samples, band_size))
    rows = shot_count * local_chan
    live = live_mask.astype(jnp.float32).reshape(rows, 1)
    spacing = samples // (2 * band_size)
    tap_delays = jnp.arange(LAGS, dtype=jnp.int32) * spacing
    lag_list = jnp.concatenate([tap_delays, gap_samples[0] + tap_delays])
    cosine, sine = delay_tables(lag_list, samples, band_size)

    def by_chunk(x):
        return x.reshape(2 * LAGS, band_size // FINE, FINE).transpose(1, 0, 2)

    cosine, sine = by_chunk(cosine), by_chunk(sine)
    turn = jnp.where(jnp.arange(2 * LAGS) < LAGS, 1.0, -1.0)[None, :, None]
    all_spec, system, rhs = front(traces, table, live, cosine, sine * turn, shot_shards, lag_shards)
    filter_rows = solve(system, rhs)
    restored = tail(all_spec, filter_rows, cosine, sine, live, table, shot_count)
    return restored.reshape(shot_count, local_chan, samples)


def solution(mesh):
    placed = (P("shot", "lag", None), P("shot", "lag"), P())
    return jax.shard_map(
        shards, mesh=mesh, in_specs=placed, out_specs=P("shot", "lag", None), check_vma=False
    )
```

```python
import functools

import jax
import jax.numpy as jnp
import ml_dtypes
import numpy as np
from jax import lax
from jax.experimental import pallas as pl
from jax.experimental.pallas import tpu as pltpu
from jax.sharding import PartitionSpec as P

LAGS=4
HALF=128
STEP=8

def mm(a, b, dims=((1,), (0,))):
    return lax.dot_general(a, b, (dims, ((), ())), precision=lax.Precision.HIGHEST, preferred_element_type=jnp.float32)


def spread(x):
    return jnp.broadcast_to(x, (STEP, HALF))


def lane_columns(tile, first):
    return [spread(tile[:, first + j : first + j + 1]) for j in range(STEP)]


def row_of(tile, i):
    return spread(tile[i : i + 1, :])


def tree_sum(terms):
    while len(terms) > 1:
        terms = [terms[i] + terms[i + 1] for i in range(0, len(terms), 2)]
    return terms[0]


def factor_half(mat):
    lane = lax.broadcasted_iota(jnp.int32, (STEP, HALF), 1)
    row = lax.broadcasted_iota(jnp.int32, (STEP, HALF), 0)
    count = HALF // STEP
    tiles = [mat[STEP * t : STEP * t + STEP, :] for t in range(count)]
    pivot_cols = lane_columns(tiles[0], 0)
    cols = {t: lane_columns(tiles[t], 0) for t in range(1, count)}
    ahead = lane_columns(tiles[1], STEP)
    done = []
    for h in range(count):
        k = STEP * h
        last = h == count - 1
        inside = (lane >= k) & (lane < k + STEP)
        p = {(i, j): row_of(pivot_cols[i], j) for i in range(STEP) for j in range(i, STEP)}
        u = [jnp.where(inside, jnp.where(lane == k + i, 1.0, 0.0), row_of(tiles[h], i)) for i in range(STEP)]
        low, inv, root = {}, [None] * STEP, [None] * STEP
        for i in range(STEP):
            root[i] = lax.rsqrt(p[i, i])
            inv[i] = root[i] * root[i]
            for j in range(i + 1, STEP):
                low[j, i] = p[i, j] * inv[i]
            for j in range(i + 1, STEP):
                for m in range(j, STEP):
                    p[j, m] = p[j, m] - low[j, i] * p[i, m]
            for j in range(i + 1, STEP):
                u[j] = u[j] - low[j, i] * u[i]
                if not last:
                    cols[h + 1][j] = cols[h + 1][j] - low[j, i] * cols[h + 1][i]
        final = u[0] * root[0]
        for i in range(1, STEP):
            final = jnp.where(row == i, u[i] * root[i], final)
        done.append(jnp.where(lane <= row + k, final, 0.0))
        if last:
            break
        scaled = [cols[h + 1][m] * inv[m] for m in range(STEP)]
        pivot_cols = [
            ahead[j] - tree_sum([scaled[m] * row_of(cols[h + 1][m], j) for m in range(STEP)])
            for j in range(STEP)
        ]
        v = [u[i] * inv[i] for i in range(STEP)]
        for t in range(h + 1, count):
            if t > h + 1:
                for i in range(STEP):
                    for j in range(i + 1, STEP):
                        cols[t][j] = cols[t][j] - low[j, i] * cols[t][i]
            update = tree_sum([cols[t][j] * v[j] for j in range(STEP)])
            tiles[t] = jnp.where(inside, 0.0, tiles[t]) - update
            if t > h + 1:
                cols[t] = lane_columns(tiles[t], k + STEP)
            if t == h + 2:
                ahead = lane_columns(tiles[t], k + 2 * STEP)
    return jnp.concatenate(done, axis=0)


def solve_kernel(corr_hbm, rhs_hbm, out_ref, aug, diag, first_inv, coupling, zero_v, load_sem):
    channels = corr_hbm.shape[1]
    order = LAGS * channels
    block = 2 * HALF
    count = order // block
    local = rhs_hbm.shape[1]

    zero_copy = pltpu.make_async_copy(corr_hbm.at[0], zero_v, load_sem.at[0])
    zero_copy.start()
    loads = []
    for lag in range(1, LAGS):
        for low in range(LAGS - lag):
            rows, cols = (low + lag) * channels, low * channels
            loads.append((corr_hbm.at[lag], aug.at[pl.ds(rows, channels), pl.ds(cols, channels)]))
    for tap in range(LAGS):
        loads.append((rhs_hbm.at[tap], aug.at[pl.ds(order, local), pl.ds(tap * channels, channels)]))
    loads = [
        pltpu.make_async_copy(source, target, load_sem.at[1 + i]) for i, (source, target) in enumerate(loads)
    ]
    for load in loads:
        load.start()
    zero_copy.wait()
    value = zero_v[...]
    same = lax.broadcasted_iota(jnp.int32, value.shape, 0) == lax.broadcasted_iota(jnp.int32, value.shape, 1)
    trace = jnp.sum(jnp.where(same, value, 0.0))
    value = value + jnp.where(same, 0.1 * (trace / channels) + 1e-06, 0.0)
    for tap in range(LAGS):
        span = slice(tap * channels, (tap + 1) * channels)
        aug[span, span] = value
    diag[...] = value[:HALF, :HALF]

    def step(half_step, carry):
        diag[...] = factor_half(diag[...])
        for b in range(count):
            o = b * block
            mid, end = o + HALF, o + block

            @pl.when(half_step == 2 * b)
            def _():
                low = mm(aug[mid:end, o:mid], diag[...], ((1,), (1,)))
                first_inv[...] = diag[...]
                coupling[...] = low
                diag[...] = aug[mid:end, mid:end] - mm(low, low, ((1,), (1,)))

            @pl.when(half_step == 2 * b + 1)
            def _():
                if b == 0:
                    for load in loads:
                        load.wait()
                top, last = first_inv[...], diag[...]
                aug[o:mid, o:mid] = top
                aug[o:mid, mid:end] = jnp.zeros((HALF, HALF), jnp.float32)
                aug[mid:end, o:mid] = -mm(last, mm(coupling[...], top))
                aug[mid:end, mid:end] = last
                aug[end:, o:end] = mm(aug[end:, o:end], aug[o:end, o:end], ((1,), (1,)))
                for c in range(end, order, block):
                    aug[c:, c : c + block] = aug[c:, c : c + block] - mm(
                        aug[c:, o:end], aug[c : c + block, o:end], ((1,), (1,))
                    )
                if end < order:
                    diag[...] = aug[end : end + HALF, end : end + HALF]

        return carry

    lax.fori_loop(0, 2 * count, step, 0)
    for b in range(count - 1, -1, -1):
        o, end = b * block, (b + 1) * block
        known = aug[order:, o:end]
        if end < order:
            known = known - mm(aug[order:, end:order], aug[end:order, o:end])
        aug[order:, o:end] = mm(known, aug[o:end, o:end])
    out_ref[...] = aug[order:, :].astype(jnp.bfloat16)


def solve(corr, rhs):
    channels = corr.shape[1]
    local = rhs.shape[1]
    order = LAGS * channels
    vm = pl.BlockSpec(memory_space=pltpu.VMEM)
    hbm = pl.BlockSpec(memory_space=pltpu.HBM)
    return pl.pallas_call(
        solve_kernel,
        out_shape=jax.ShapeDtypeStruct((local, order), jnp.bfloat16),
        in_specs=[hbm, hbm],
        out_specs=vm,
        scratch_shapes=[
            pltpu.VMEM((order + local, order), jnp.float32),
            pltpu.VMEM((HALF, HALF), jnp.float32),
            pltpu.VMEM((HALF, HALF), jnp.float32),
            pltpu.VMEM((HALF, HALF), jnp.float32),
            pltpu.VMEM((channels, channels), jnp.float32),
            pltpu.SemaphoreType.DMA((1 + LAGS * (LAGS - 1) // 2 + LAGS,)),
        ],
        compiler_params=pltpu.CompilerParams(vmem_limit_bytes=63 << 20),
        name="block_solve",
    )(corr, rhs)


MESH = pl.DeviceIdType.MESH
FINE = 128


def dft_table(samples, band_size):
    times = np.arange(samples // 2, dtype=np.int64)
    harmonic = np.arange(1, band_size + 1, dtype=np.int64)
    phase = (times[:, None] * harmonic[None, :]) % (2 * samples)
    circle = np.arange(2 * samples).astype(np.float32) * np.float32(np.pi / samples)
    cosines = np.cos(circle.astype(np.float64)).astype(np.float32).astype(ml_dtypes.bfloat16)[phase]
    sines = np.sin(circle.astype(np.float64)).astype(np.float32).astype(ml_dtypes.bfloat16)[phase]
    pair = np.stack([cosines.reshape(samples // 2, -1, FINE), sines.reshape(samples // 2, -1, FINE)], axis=2)
    return pair.reshape(samples // 2, 2 * band_size)


def low_bit(value):
    return value & -value


def quarter_turn(c, shape):
    harmonic = (lax.broadcasted_iota(jnp.int32, shape, 1) + (c * FINE + 1)) & 3
    cosine = jnp.where(harmonic == 0, 1.0, jnp.where(harmonic == 2, -1.0, 0.0))
    sine = jnp.where(harmonic == 1, 1.0, jnp.where(harmonic == 3, -1.0, 0.0))
    return cosine, sine


def front_kernel(
    shape, scales, x_hbm, table_hbm, live_ref, cos_ref, sin_ref, spec_ref, sys_ref, rhs_ref,
    x_v, tab_v, all_v, rot_v, acc_v, part_v, recv_v, full_v, rfull_v,
    x_sem, tab_sem, out_sem, spec_send, spec_recv, red_send, red_recv, piece_send, piece_recv, lag_send, lag_recv,
):
    shots, shot_shards, lag_shards = shape
    rows, samples = x_v.shape[0] // 2, x_v.shape[1]
    local = rows // shots
    chunks = all_v.shape[0]
    channels = all_v.shape[1]
    wide = 2 * FINE
    blocks = x_sem.shape[0]
    block = samples // blocks
    my_shot, my_lag = lax.axis_index("shot"), lax.axis_index("lag")
    bits = [1 << i for i in range(lag_shards.bit_length() - 2, -1, -1)]
    deltas = sorted(range(1, lag_shards), key=lambda d: -low_bit(d))
    near = [d for d in deltas if d < lag_shards // 2]
    far = [d for d in deltas if d >= lag_shards // 2]
    half = channels // 2
    my_half = my_lag // (lag_shards // 2)

    def x_copy(b, side):
        span = pl.ds(b * block, block)
        return pltpu.make_async_copy(
            x_hbm.at[:, pl.ds(side * samples + b * block, block)],
            x_v.at[pl.ds(side * rows, rows), span], x_sem.at[b, side],
        )

    def first_copy(b):
        span = pl.ds(b * block, block)
        return pltpu.make_async_copy(
            table_hbm.at[span, pl.ds(0, wide)], tab_v.at[0, span], tab_sem.at[chunks + b]
        )

    def table_copy(c):
        return pltpu.make_async_copy(
            table_hbm.at[:, pl.ds(pl.multiple_of(c * wide, wide), wide)], tab_v.at[c], tab_sem.at[c]
        )

    for b in range(blocks):
        first_copy(b).start()
        for side in range(2):
            x_copy(b, side).start()

    barrier = pltpu.get_barrier_semaphore()
    for j in range(1, shot_shards):
        pl.semaphore_signal(barrier, inc=1, device_id=(my_shot ^ j, my_lag), device_id_type=MESH)
    for v in bits:
        pl.semaphore_signal(barrier, inc=1, device_id=(my_shot, my_lag ^ v), device_id_type=MESH)

    def rows_of(lag):
        return pl.ds(pl.multiple_of(lag * local, local), local)

    def spec_copy(c, delta, arriving=False):
        v = low_bit(delta)
        span = rows_of(my_lag ^ (delta if arriving else delta ^ v))
        return pltpu.make_async_remote_copy(
            src_ref=all_v.at[c, span], dst_ref=all_v.at[c, span],
            send_sem=spec_send.at[c, delta], recv_sem=spec_recv.at[c, delta],
            device_id=(my_shot, my_lag ^ v), device_id_type=MESH,
        )

    def forward(c, group):
        for delta in group:
            if low_bit(delta) > 1:
                spec_copy(c, delta, True).wait_recv()
                for v in bits:
                    if v < low_bit(delta):
                        spec_copy(c, delta | v).start()

    def settle(c, group):
        for delta in group:
            if low_bit(delta) == 1:
                spec_copy(c, delta, True).wait_recv()

    def transform(c, loaded):
        total = None
        for b in range(blocks):
            if loaded is not None:
                loaded(b)
            term = jnp.dot(
                x_v[:, b * block : (b + 1) * block], tab_v[c, b * block : (b + 1) * block, :],
                preferred_element_type=jnp.float32,
            )
            total = term if total is None else total + term
        turn_cos, turn_sin = quarter_turn(c, (1, FINE))
        early, late = total[:rows], total[rows:]
        live = live_ref[...].astype(jnp.float32).T
        real = early[:, :FINE] + (late[:, :FINE] * turn_cos - late[:, FINE:] * turn_sin)
        imag = early[:, FINE:] + (late[:, FINE:] * turn_cos + late[:, :FINE] * turn_sin)
        for s in range(shots):
            span, o = slice(s * local, (s + 1) * local), s * wide
            all_v[c, rows_of(my_lag), o : o + FINE] = (real[span] * live[:, s : s + 1]).astype(jnp.bfloat16)
            all_v[c, rows_of(my_lag), o + FINE : o + wide] = (imag[span] * live[:, s : s + 1]).astype(jnp.bfloat16)

    def send_own(c):
        for v in bits:
            spec_copy(c, v).start()

    def rotate(c):
        own = all_v[c, rows_of(my_lag), :].astype(jnp.float32)
        for k in range(2 * LAGS):
            cosine, sine = cos_ref[c, k : k + 1, :], sin_ref[c, k : k + 1, :]
            for s in range(shots):
                o = s * wide
                real, imag = own[:, o : o + FINE], own[:, o + FINE : o + wide]
                rot_v[c, k * local : (k + 1) * local, o : o + FINE] = (real * cosine - imag * sine).astype(jnp.bfloat16)
                rot_v[c, k * local : (k + 1) * local, o + FINE : o + wide] = (imag * cosine + real * sine).astype(jnp.bfloat16)

    def correlate(c, h, side):
        acc_v[h] = acc_v[h] + lax.dot_general(
            rot_v[c], all_v[c, pl.ds(pl.multiple_of(side * half, half), half), :],
            (((1,), (1,)), ((), ())), preferred_element_type=jnp.float32,
        )

    def first_loaded(b):
        first_copy(b).wait()
        for side in range(2):
            x_copy(b, side).wait()
        if b + 1 == blocks:
            for c in range(1, chunks):
                table_copy(c).start()

    acc_v[...] = jnp.zeros_like(acc_v)
    transform(0, first_loaded)
    pl.semaphore_wait(barrier, shot_shards - 1 + len(bits))
    send_own(0)

    def transform_step(c, carry):
        table_copy(c).wait()
        rotate(c - 1)
        transform(c, None)
        send_own(c)
        return carry

    lax.fori_loop(1, chunks, transform_step, 0)
    rotate(chunks - 1)

    def near_step(c, carry):
        forward(c, near)
        settle(c, near)
        correlate(c, 0, my_half)
        return carry

    lax.fori_loop(0, chunks, near_step, 0)

    piece = part_v.shape[2]

    def reduce_copy(e, j):
        return pltpu.make_async_remote_copy(
            src_ref=part_v.at[e, my_shot ^ j], dst_ref=recv_v.at[e, j],
            send_sem=red_send.at[e, j], recv_sem=red_recv.at[e, j],
            device_id=(my_shot ^ j, my_lag), device_id_type=MESH,
        )

    def scatter(h):
        for g in range(2):
            for p in range(shot_shards):
                top = g * LAGS * local + p * piece
                part_v[2 * g + h, p] = acc_v[h, top : top + piece, :]
        for g in range(2):
            for j in range(1, shot_shards):
                reduce_copy(2 * g + h, j).start()

    def piece_copy(e, j, arriving=False):
        hop = 1 if j % 2 else j
        owner = my_shot ^ (j if arriving else j ^ hop)
        ref = full_v.at[my_lag, e, owner] if e < 2 else rfull_v.at[e - 2, owner]
        return pltpu.make_async_remote_copy(
            src_ref=ref, dst_ref=ref,
            send_sem=piece_send.at[e, j], recv_sem=piece_recv.at[e, j],
            device_id=(my_shot ^ hop, my_lag), device_id_type=MESH,
        )

    def lag_copy(e, j, delta, arriving=False):
        v = low_bit(delta)
        ref = full_v.at[my_lag ^ (delta if arriving else delta ^ v), e, my_shot ^ j]
        return pltpu.make_async_remote_copy(
            src_ref=ref, dst_ref=ref,
            send_sem=lag_send.at[e, j, delta], recv_sem=lag_recv.at[e, j, delta],
            device_id=(my_shot, my_lag ^ v), device_id_type=MESH,
        )

    def reduce(e):
        total = part_v[e, my_shot]
        for j in range(1, shot_shards):
            reduce_copy(e, j).wait_recv()
            total = total + recv_v[e, j]
        total = total * scales[0] * scales[1]
        if e < 2:
            full_v[my_lag, e, my_shot] = total
        else:
            rfull_v[e - 2, my_shot] = total
        for j in [*range(2, shot_shards, 2), 1]:
            piece_copy(e, j).start()

    def collect(e):
        for j in range(2, shot_shards, 2):
            piece_copy(e, j, True).wait_recv()
            piece_copy(e, j | 1).start()

    def share(e, collected):
        for j in [*range(0, shot_shards, 2), *range(1, shot_shards, 2)]:
            if j % 2 or (j and not collected):
                piece_copy(e, j, True).wait_recv()
            if j and j % 2 == 0 and not collected:
                piece_copy(e, j | 1).start()
            for v in bits:
                lag_copy(e, j, v).start()

    def relay(e):
        for j in range(shot_shards):
            for delta in deltas:
                if low_bit(delta) > 1:
                    lag_copy(e, j, delta, True).wait_recv()
                    for v in bits:
                        if v < low_bit(delta):
                            lag_copy(e, j, delta | v).start()

    def far_step(c, carry):
        forward(c, far)
        settle(c, far)
        correlate(c, 1, 1 - my_half)
        return carry

    def out_copy(c):
        return pltpu.make_async_copy(all_v.at[c], spec_ref.at[c], out_sem.at[c])

    scatter(0)
    lax.fori_loop(0, chunks - 1, far_step, 0)
    reduce(0)
    far_step(chunks - 1, 0)
    scatter(1)
    for c in range(chunks):
        out_copy(c).start()
    share(0, False)
    reduce(2)
    reduce(1)
    share(1, False)
    reduce(3)
    relay(0)
    collect(2)
    collect(3)
    relay(1)
    for e in (2, 3):
        for j in range(1, shot_shards, 2):
            piece_copy(e, j, True).wait_recv()
    unit = min(piece, local)
    for h in range(2):
        side = my_half if h == 0 else 1 - my_half
        lanes = pl.ds(pl.multiple_of(side * half, half), half)
        for p in range(shot_shards):
            for r in range(0, piece, unit):
                k, a = (p * piece + r) // local, (p * piece + r) % local
                rhs_ref[k, a : a + unit, lanes] = rfull_v[h, p, r : r + unit]
    for e in range(2):
        for j in range(shot_shards):
            for delta in deltas:
                if low_bit(delta) == 1:
                    lag_copy(e, j, delta, True).wait_recv()
    for q in range(lag_shards):
        for h in range(2):
            lane = ((q // (lag_shards // 2)) ^ h) * half
            for p in range(shot_shards):
                for r in range(0, piece, unit):
                    k, a = (p * piece + r) // local, (p * piece + r) % local + q * local
                    sys_ref[k, a : a + unit, lane : lane + half] = full_v[q, h, p, r : r + unit]
    for c in range(chunks):
        out_copy(c).wait()
        for delta in deltas:
            spec_copy(c, delta).wait_send()
    for e in range(4):
        for j in range(1, shot_shards):
            reduce_copy(e, j).wait_send()
            piece_copy(e, j).wait_send()
    for e in range(2):
        for j in range(shot_shards):
            for delta in deltas:
                lag_copy(e, j, delta).wait_send()


def front(traces, table, live, cosine, sine, shot_shards, lag_shards):
    shots, local, samples = traces.shape
    rows = shots * local
    width = table.shape[1]
    chunks = width // (2 * FINE)
    channels = local * lag_shards
    half = channels // 2
    blocks = 4
    piece = LAGS * local // shot_shards
    total_shots = shots * shot_shards
    scales = (1.0 / samples, 1.0 / (samples * total_shots))
    hbm = pl.BlockSpec(memory_space=pltpu.HBM)
    vm = pl.BlockSpec(memory_space=pltpu.VMEM)
    sem = pltpu.SemaphoreType.DMA
    return pl.pallas_call(
        functools.partial(front_kernel, (shots, shot_shards, lag_shards), scales),
        out_shape=(
            jax.ShapeDtypeStruct((chunks, channels, shots * 2 * FINE), jnp.bfloat16),
            jax.ShapeDtypeStruct((LAGS, channels, channels), jnp.float32),
            jax.ShapeDtypeStruct((LAGS, local, channels), jnp.float32),
        ),
        in_specs=[hbm, hbm, vm, vm, vm],
        out_specs=(hbm, vm, vm),
        scratch_shapes=[
            pltpu.VMEM((2 * rows, samples // 2), jnp.bfloat16),
            pltpu.VMEM((chunks, samples // 2, 2 * FINE), jnp.bfloat16),
            pltpu.VMEM((chunks, channels, shots * 2 * FINE), jnp.bfloat16),
            pltpu.VMEM((chunks, 2 * LAGS * local, shots * 2 * FINE), jnp.bfloat16),
            pltpu.VMEM((2, 2 * LAGS * local, half), jnp.float32),
            pltpu.VMEM((4, shot_shards, piece, half), jnp.float32),
            pltpu.VMEM((4, shot_shards, piece, half), jnp.float32),
            pltpu.VMEM((lag_shards, 2, shot_shards, piece, half), jnp.float32),
            pltpu.VMEM((2, shot_shards, piece, half), jnp.float32),
            sem((blocks, 2)),
            sem((chunks + blocks,)),
            sem((chunks,)),
            sem((chunks, lag_shards)),
            sem((chunks, lag_shards)),
            sem((4, shot_shards)),
            sem((4, shot_shards)),
            sem((4, shot_shards)),
            sem((4, shot_shards)),
            sem((2, shot_shards, lag_shards)),
            sem((2, shot_shards, lag_shards)),
        ],
        compiler_params=pltpu.CompilerParams(
            collective_id=0, has_side_effects=True, vmem_limit_bytes=56 << 20
        ),
        name="front",
    )(traces.reshape(rows, samples), table, live, cosine, sine)


def tail_kernel(
    shots, scale, spec_hbm, filter_ref, cos_ref, sin_ref, live_ref, table_hbm, out_hbm,
    spec_v, tab_v, err_v, stage_v, spec_sem, tab_sem, out_sem,
):
    chunks, channels = spec_v.shape[:2]
    local = filter_ref.shape[0]
    rows = shots * local
    wide = 2 * FINE
    steps, step = tab_v.shape[:2]
    my_lag = lax.axis_index("lag")

    def spec_copy(c):
        return pltpu.make_async_copy(spec_hbm.at[c], spec_v.at[c], spec_sem.at[c])

    def table_copy(t):
        span = pl.ds(pl.multiple_of(t * step, step), step)
        return pltpu.make_async_copy(table_hbm.at[span], tab_v.at[t], tab_sem.at[t])

    def out_copy(t, side):
        span = pl.ds(pl.multiple_of((side * steps + t) * step, step), step)
        slot = lax.rem(t, 2)
        return pltpu.make_async_copy(
            stage_v.at[slot, pl.ds(side * rows, rows)], out_hbm.at[:, span], out_sem.at[slot, side]
        )

    for c in range(chunks):
        spec_copy(c).start()
    taps = jnp.concatenate(
        [filter_ref[:, j * channels : (j + 1) * channels] for j in range(LAGS)], axis=0
    )
    for c in range(chunks):
        spec_copy(c).wait()
        if c == chunks // 2:
            for t in range(steps):
                table_copy(t).start()
        own = spec_v[c, pl.ds(pl.multiple_of(my_lag * local, local), local), :].astype(jnp.float32)
        turn_cos, turn_sin = quarter_turn(c, (1, FINE))
        for s in range(shots):
            o = s * wide
            mixed = jnp.dot(taps, spec_v[c, :, o : o + wide], preferred_element_type=jnp.float32)
            real, imag = own[:, o : o + FINE], own[:, o + FINE : o + wide]
            for j in range(LAGS):
                cosine, sine = cos_ref[c, LAGS + j : LAGS + j + 1, :], sin_ref[c, LAGS + j : LAGS + j + 1, :]
                a = mixed[j * local : (j + 1) * local, :FINE]
                b = mixed[j * local : (j + 1) * local, FINE:]
                real = real - (a * cosine - b * sine)
                imag = imag - (b * cosine + a * sine)
            top, lane = s * local, c * wide
            err_v[top : top + local, lane : lane + FINE] = real.astype(jnp.bfloat16)
            err_v[top : top + local, lane + FINE : lane + wide] = imag.astype(jnp.bfloat16)
            top = rows + top
            err_v[top : top + local, lane : lane + FINE] = (real * turn_cos + imag * turn_sin).astype(jnp.bfloat16)
            err_v[top : top + local, lane + FINE : lane + wide] = (imag * turn_cos - real * turn_sin).astype(jnp.bfloat16)
    live = live_ref[...].astype(jnp.float32).T * scale
    live = jnp.concatenate([live[:, s : s + 1] for s in range(shots)], axis=0)

    def back_step(t, carry):
        table_copy(t).wait()

        @pl.when(t >= 2)
        def _():
            for side in range(2):
                out_copy(t - 2, side).wait()

        value = lax.dot_general(
            err_v[...], tab_v[t], (((1,), (1,)), ((), ())), preferred_element_type=jnp.float32
        )
        slot = lax.rem(t, 2)
        for side in range(2):
            stage_v[slot, side * rows : (side + 1) * rows, :] = (
                value[side * rows : (side + 1) * rows] * live
            ).astype(jnp.bfloat16)
            out_copy(t, side).start()
        return carry

    lax.fori_loop(0, steps, back_step, 0)
    for t in range(max(steps - 2, 0), steps):
        for side in range(2):
            out_copy(t, side).wait()


def tail(all_spec, filter_rows, cosine, sine, live, table, shots):
    samples, depth = table.shape
    rows = live.size
    step = min(512, samples)
    hbm = pl.BlockSpec(memory_space=pltpu.HBM)
    vm = pl.BlockSpec(memory_space=pltpu.VMEM)
    return pl.pallas_call(
        functools.partial(tail_kernel, shots, 0.5 / samples),
        out_shape=jax.ShapeDtypeStruct((rows, 2 * samples), jnp.bfloat16),
        in_specs=[hbm, vm, vm, vm, vm, hbm],
        out_specs=hbm,
        scratch_shapes=[
            pltpu.VMEM(all_spec.shape, jnp.bfloat16),
            pltpu.VMEM((samples // step, step, depth), jnp.bfloat16),
            pltpu.VMEM((2 * rows, depth), jnp.bfloat16),
            pltpu.VMEM((2, 2 * rows, step), jnp.bfloat16),
            pltpu.SemaphoreType.DMA((all_spec.shape[0],)),
            pltpu.SemaphoreType.DMA((samples // step,)),
            pltpu.SemaphoreType.DMA((2, 2)),
        ],
        compiler_params=pltpu.CompilerParams(vmem_limit_bytes=62 << 20),
        name="tail",
    )(all_spec, filter_rows, cosine, sine, live, table)


def delay_tables(delays, samples, band_size):
    harmonic = jnp.arange(1, band_size + 1, dtype=jnp.int32)
    phase = delays[:, None] * harmonic[None, :] % (2 * samples)
    angle = phase.astype(jnp.float32) * (jnp.pi / samples)
    return (jnp.cos(angle), jnp.sin(angle))


def shards(traces, live_mask, gap_samples):
    shot_count, local_chan, samples = traces.shape
    band_size = samples // 16
    shot_shards, lag_shards = lax.axis_size("shot"), lax.axis_size("lag")
    table = jnp.asarray(dft_table(samples, band_size))
    spacing = samples // (2 * band_size)
    tap_delays = jnp.arange(LAGS, dtype=jnp.int32) * spacing
    lag_list = jnp.concatenate([tap_delays, gap_samples[0] + tap_delays])
    cosine, sine = delay_tables(lag_list, samples, band_size)

    def by_chunk(x):
        return x.reshape(2 * LAGS, band_size // FINE, FINE).transpose(1, 0, 2)

    cosine, sine = by_chunk(cosine), by_chunk(sine)
    turn = jnp.where(jnp.arange(2 * LAGS) < LAGS, 1.0, -1.0)[None, :, None]
    all_spec, system, rhs = front(traces, table, live_mask, cosine, sine * turn, shot_shards, lag_shards)
    filter_rows = solve(system, rhs)
    restored = tail(all_spec, filter_rows, cosine, sine, live_mask, table, shot_count)
    return restored.reshape(shot_count, local_chan, samples)


def solution(mesh):
    placed = (P("shot", "lag", None), P("shot", "lag"), P())
    return jax.shard_map(
        shards, mesh=mesh, in_specs=placed, out_specs=P("shot", "lag", None), check_vma=False
    )
```

```python
import functools

import jax
import jax.numpy as jnp
import ml_dtypes
import numpy as np
from jax import lax
from jax.experimental import pallas as pl
from jax.experimental.pallas import tpu as pltpu
from jax.sharding import PartitionSpec as P

LAGS=4
HALF=128
STEP=8

def mm(a, b, dims=((1,), (0,))):
    return lax.dot_general(a, b, (dims, ((), ())), precision=lax.Precision.HIGHEST, preferred_element_type=jnp.float32)


def spread(x):
    return jnp.broadcast_to(x, (STEP, HALF))


def lane_columns(tile, first):
    return [
        jnp.take_along_axis(tile, jnp.full(tile.shape, first + j, jnp.int32), axis=1) for j in range(STEP)
    ]


def row_of(tile, i):
    return spread(tile[i : i + 1, :])


def tree_sum(terms):
    while len(terms) > 1:
        terms = [terms[i] + terms[i + 1] for i in range(0, len(terms), 2)]
    return terms[0]


def factor_half(mat):
    lane = lax.broadcasted_iota(jnp.int32, (STEP, HALF), 1)
    row = lax.broadcasted_iota(jnp.int32, (STEP, HALF), 0)
    count = HALF // STEP
    tiles = [mat[STEP * t : STEP * t + STEP, :] for t in range(count)]
    pivot_cols = lane_columns(tiles[0], 0)
    cols = {t: lane_columns(tiles[t], 0) for t in range(1, count)}
    ahead = lane_columns(tiles[1], STEP)
    done = []
    for h in range(count):
        k = STEP * h
        last = h == count - 1
        inside = (lane >= k) & (lane < k + STEP)
        p = {(i, j): row_of(pivot_cols[i], j) for i in range(STEP) for j in range(i, STEP)}
        u = [jnp.where(inside, jnp.where(lane == k + i, 1.0, 0.0), row_of(tiles[h], i)) for i in range(STEP)]
        low, inv, root = {}, [None] * STEP, [None] * STEP
        for i in range(STEP):
            root[i] = lax.rsqrt(p[i, i])
            inv[i] = root[i] * root[i]
            for j in range(i + 1, STEP):
                low[j, i] = p[i, j] * inv[i]
            for j in range(i + 1, STEP):
                for m in range(j, STEP):
                    p[j, m] = p[j, m] - low[j, i] * p[i, m]
            for j in range(i + 1, STEP):
                u[j] = u[j] - low[j, i] * u[i]
                if not last:
                    cols[h + 1][j] = cols[h + 1][j] - low[j, i] * cols[h + 1][i]
        final = u[0] * root[0]
        for i in range(1, STEP):
            final = jnp.where(row == i, u[i] * root[i], final)
        done.append(jnp.where(lane <= row + k, final, 0.0))
        if last:
            break
        scaled = [cols[h + 1][m] * inv[m] for m in range(STEP)]
        pivot_cols = [
            ahead[j] - tree_sum([scaled[m] * row_of(cols[h + 1][m], j) for m in range(STEP)])
            for j in range(STEP)
        ]
        v = [u[i] * inv[i] for i in range(STEP)]
        for t in range(h + 1, count):
            if t > h + 1:
                for i in range(STEP):
                    for j in range(i + 1, STEP):
                        cols[t][j] = cols[t][j] - low[j, i] * cols[t][i]
            update = tree_sum([cols[t][j] * v[j] for j in range(STEP)])
            tiles[t] = jnp.where(inside, 0.0, tiles[t]) - update
            if t > h + 1:
                cols[t] = lane_columns(tiles[t], k + STEP)
            if t == h + 2:
                ahead = lane_columns(tiles[t], k + 2 * STEP)
    return jnp.concatenate(done, axis=0)


def solve_kernel(corr_hbm, rhs_hbm, out_ref, aug, diag, first_inv, coupling, zero_v, load_sem):
    channels = corr_hbm.shape[1]
    order = LAGS * channels
    block = 2 * HALF
    count = order // block
    local = rhs_hbm.shape[1]

    zero_copy = pltpu.make_async_copy(corr_hbm.at[0], zero_v, load_sem.at[0])
    zero_copy.start()
    loads = []
    for lag in range(1, LAGS):
        for low in range(LAGS - lag):
            rows, cols = (low + lag) * channels, low * channels
            loads.append((corr_hbm.at[lag], aug.at[pl.ds(rows, channels), pl.ds(cols, channels)]))
    for tap in range(LAGS):
        loads.append((rhs_hbm.at[tap], aug.at[pl.ds(order, local), pl.ds(tap * channels, channels)]))
    loads = [
        pltpu.make_async_copy(source, target, load_sem.at[1 + i]) for i, (source, target) in enumerate(loads)
    ]
    for load in loads:
        load.start()
    zero_copy.wait()
    value = zero_v[...]
    same = lax.broadcasted_iota(jnp.int32, value.shape, 0) == lax.broadcasted_iota(jnp.int32, value.shape, 1)
    trace = jnp.sum(jnp.where(same, value, 0.0))
    value = value + jnp.where(same, 0.1 * (trace / channels) + 1e-06, 0.0)
    for tap in range(LAGS):
        span = slice(tap * channels, (tap + 1) * channels)
        aug[span, span] = value
    diag[...] = value[:HALF, :HALF]

    def step(half_step, carry):
        diag[...] = factor_half(diag[...])
        for b in range(count):
            o = b * block
            mid, end = o + HALF, o + block

            @pl.when(half_step == 2 * b)
            def _():
                low = mm(aug[mid:end, o:mid], diag[...], ((1,), (1,)))
                first_inv[...] = diag[...]
                coupling[...] = low
                diag[...] = aug[mid:end, mid:end] - mm(low, low, ((1,), (1,)))

            @pl.when(half_step == 2 * b + 1)
            def _():
                if b == 0:
                    for load in loads:
                        load.wait()
                top, last = first_inv[...], diag[...]
                aug[o:mid, o:mid] = top
                aug[o:mid, mid:end] = jnp.zeros((HALF, HALF), jnp.float32)
                aug[mid:end, o:mid] = -mm(last, mm(coupling[...], top))
                aug[mid:end, mid:end] = last
                aug[end:, o:end] = mm(aug[end:, o:end], aug[o:end, o:end], ((1,), (1,)))
                for c in range(end, order, block):
                    aug[c:, c : c + block] = aug[c:, c : c + block] - mm(
                        aug[c:, o:end], aug[c : c + block, o:end], ((1,), (1,))
                    )
                if end < order:
                    diag[...] = aug[end : end + HALF, end : end + HALF]

        return carry

    lax.fori_loop(0, 2 * count, step, 0)
    for b in range(count - 1, -1, -1):
        o, end = b * block, (b + 1) * block
        known = aug[order:, o:end]
        if end < order:
            known = known - mm(aug[order:, end:order], aug[end:order, o:end])
        aug[order:, o:end] = mm(known, aug[o:end, o:end])
    out_ref[...] = aug[order:, :].astype(jnp.bfloat16)


def solve(corr, rhs):
    channels = corr.shape[1]
    local = rhs.shape[1]
    order = LAGS * channels
    vm = pl.BlockSpec(memory_space=pltpu.VMEM)
    hbm = pl.BlockSpec(memory_space=pltpu.HBM)
    return pl.pallas_call(
        solve_kernel,
        out_shape=jax.ShapeDtypeStruct((local, order), jnp.bfloat16),
        in_specs=[hbm, hbm],
        out_specs=vm,
        scratch_shapes=[
            pltpu.VMEM((order + local, order), jnp.float32),
            pltpu.VMEM((HALF, HALF), jnp.float32),
            pltpu.VMEM((HALF, HALF), jnp.float32),
            pltpu.VMEM((HALF, HALF), jnp.float32),
            pltpu.VMEM((channels, channels), jnp.float32),
            pltpu.SemaphoreType.DMA((1 + LAGS * (LAGS - 1) // 2 + LAGS,)),
        ],
        compiler_params=pltpu.CompilerParams(vmem_limit_bytes=63 << 20),
        name="block_solve",
    )(corr, rhs)


MESH = pl.DeviceIdType.MESH
FINE = 128


def dft_table(samples, band_size):
    times = np.arange(samples // 2, dtype=np.int64)
    harmonic = np.arange(1, band_size + 1, dtype=np.int64)
    phase = (times[:, None] * harmonic[None, :]) % (2 * samples)
    circle = np.arange(2 * samples).astype(np.float32) * np.float32(np.pi / samples)
    cosines = np.cos(circle.astype(np.float64)).astype(np.float32).astype(ml_dtypes.bfloat16)[phase]
    sines = np.sin(circle.astype(np.float64)).astype(np.float32).astype(ml_dtypes.bfloat16)[phase]
    pair = np.stack([cosines.reshape(samples // 2, -1, FINE), sines.reshape(samples // 2, -1, FINE)], axis=2)
    return pair.reshape(samples // 2, 2 * band_size)


def low_bit(value):
    return value & -value


def quarter_turn(c, shape):
    harmonic = (lax.broadcasted_iota(jnp.int32, shape, 1) + (c * FINE + 1)) & 3
    cosine = jnp.where(harmonic == 0, 1.0, jnp.where(harmonic == 2, -1.0, 0.0))
    sine = jnp.where(harmonic == 1, 1.0, jnp.where(harmonic == 3, -1.0, 0.0))
    return cosine, sine


def front_kernel(
    shape, scales, x_hbm, table_hbm, live_ref, cos_ref, sin_ref, spec_ref, sys_ref, rhs_ref,
    x_v, tab_v, all_v, rot_v, acc_v, part_v, recv_v, full_v, rfull_v,
    x_sem, tab_sem, out_sem, spec_send, spec_recv, red_send, red_recv, piece_send, piece_recv, lag_send, lag_recv,
):
    shots, shot_shards, lag_shards = shape
    rows, samples = x_v.shape[0] // 2, x_v.shape[1]
    local = rows // shots
    chunks = all_v.shape[0]
    channels = all_v.shape[1]
    wide = 2 * FINE
    blocks = x_sem.shape[0]
    block = samples // blocks
    my_shot, my_lag = lax.axis_index("shot"), lax.axis_index("lag")
    bits = [1 << i for i in range(lag_shards.bit_length() - 2, -1, -1)]
    deltas = sorted(range(1, lag_shards), key=lambda d: -low_bit(d))
    near = [d for d in deltas if d < lag_shards // 2]
    far = [d for d in deltas if d >= lag_shards // 2]
    half = channels // 2
    my_half = my_lag // (lag_shards // 2)

    def x_copy(b, side):
        span = pl.ds(b * block, block)
        return pltpu.make_async_copy(
            x_hbm.at[:, pl.ds(side * samples + b * block, block)],
            x_v.at[pl.ds(side * rows, rows), span], x_sem.at[b, side],
        )

    def first_copy(b):
        span = pl.ds(b * block, block)
        return pltpu.make_async_copy(
            table_hbm.at[span, pl.ds(0, wide)], tab_v.at[0, span], tab_sem.at[chunks + b]
        )

    def table_copy(c):
        return pltpu.make_async_copy(
            table_hbm.at[:, pl.ds(pl.multiple_of(c * wide, wide), wide)], tab_v.at[c], tab_sem.at[c]
        )

    for b in range(blocks):
        first_copy(b).start()
        for side in range(2):
            x_copy(b, side).start()

    barrier = pltpu.get_barrier_semaphore()
    for j in range(1, shot_shards):
        pl.semaphore_signal(barrier, inc=1, device_id=(my_shot ^ j, my_lag), device_id_type=MESH)
    for v in bits:
        pl.semaphore_signal(barrier, inc=1, device_id=(my_shot, my_lag ^ v), device_id_type=MESH)

    def rows_of(lag):
        return pl.ds(pl.multiple_of(lag * local, local), local)

    def spec_copy(c, delta, arriving=False):
        v = low_bit(delta)
        span = rows_of(my_lag ^ (delta if arriving else delta ^ v))
        return pltpu.make_async_remote_copy(
            src_ref=all_v.at[c, span], dst_ref=all_v.at[c, span],
            send_sem=spec_send.at[c, delta], recv_sem=spec_recv.at[c, delta],
            device_id=(my_shot, my_lag ^ v), device_id_type=MESH,
        )

    def forward(c, group):
        for delta in group:
            if low_bit(delta) > 1:
                spec_copy(c, delta, True).wait_recv()
                for v in bits:
                    if v < low_bit(delta):
                        spec_copy(c, delta | v).start()

    def settle(c, group):
        for delta in group:
            if low_bit(delta) == 1:
                spec_copy(c, delta, True).wait_recv()

    def transform(c, loaded):
        total = None
        for b in range(blocks):
            if loaded is not None:
                loaded(b)
            term = jnp.dot(
                x_v[:, b * block : (b + 1) * block], tab_v[c, b * block : (b + 1) * block, :],
                preferred_element_type=jnp.float32,
            )
            total = term if total is None else total + term
        turn_cos, turn_sin = quarter_turn(c, (1, FINE))
        early, late = total[:rows], total[rows:]
        live = live_ref[...].astype(jnp.float32).T
        real = early[:, :FINE] + (late[:, :FINE] * turn_cos - late[:, FINE:] * turn_sin)
        imag = early[:, FINE:] + (late[:, FINE:] * turn_cos + late[:, :FINE] * turn_sin)
        for s in range(shots):
            span, o = slice(s * local, (s + 1) * local), s * wide
            all_v[c, rows_of(my_lag), o : o + FINE] = (real[span] * live[:, s : s + 1]).astype(jnp.bfloat16)
            all_v[c, rows_of(my_lag), o + FINE : o + wide] = (imag[span] * live[:, s : s + 1]).astype(jnp.bfloat16)

    def send_own(c):
        for v in bits:
            spec_copy(c, v).start()

    def rotate(c):
        own = all_v[c, rows_of(my_lag), :].astype(jnp.float32)
        for k in range(2 * LAGS):
            cosine, sine = cos_ref[c, k : k + 1, :], sin_ref[c, k : k + 1, :]
            for s in range(shots):
                o = s * wide
                real, imag = own[:, o : o + FINE], own[:, o + FINE : o + wide]
                rot_v[c, k * local : (k + 1) * local, o : o + FINE] = (real * cosine - imag * sine).astype(jnp.bfloat16)
                rot_v[c, k * local : (k + 1) * local, o + FINE : o + wide] = (imag * cosine + real * sine).astype(jnp.bfloat16)

    def correlate(c, h, side):
        acc_v[h] = acc_v[h] + lax.dot_general(
            rot_v[c], all_v[c, pl.ds(pl.multiple_of(side * half, half), half), :],
            (((1,), (1,)), ((), ())), preferred_element_type=jnp.float32,
        )

    def first_loaded(b):
        first_copy(b).wait()
        for side in range(2):
            x_copy(b, side).wait()
        if b + 1 == blocks:
            for c in range(1, chunks):
                table_copy(c).start()

    acc_v[...] = jnp.zeros_like(acc_v)
    transform(0, first_loaded)
    pl.semaphore_wait(barrier, shot_shards - 1 + len(bits))
    send_own(0)

    def transform_step(c, carry):
        table_copy(c).wait()
        rotate(c - 1)
        transform(c, None)
        send_own(c)
        return carry

    lax.fori_loop(1, chunks, transform_step, 0)
    rotate(chunks - 1)

    def near_step(c, carry):
        forward(c, near)
        settle(c, near)
        correlate(c, 0, my_half)
        return carry

    lax.fori_loop(0, chunks, near_step, 0)

    piece = part_v.shape[2]

    def reduce_copy(e, j):
        return pltpu.make_async_remote_copy(
            src_ref=part_v.at[e, my_shot ^ j], dst_ref=recv_v.at[e, j],
            send_sem=red_send.at[e, j], recv_sem=red_recv.at[e, j],
            device_id=(my_shot ^ j, my_lag), device_id_type=MESH,
        )

    def scatter(h):
        for g in range(2):
            for p in range(shot_shards):
                top = g * LAGS * local + p * piece
                part_v[2 * g + h, p] = acc_v[h, top : top + piece, :]
        for g in range(2):
            for j in range(1, shot_shards):
                reduce_copy(2 * g + h, j).start()

    def piece_copy(e, j, arriving=False):
        hop = 1 if j % 2 else j
        owner = my_shot ^ (j if arriving else j ^ hop)
        ref = full_v.at[my_lag, e, owner] if e < 2 else rfull_v.at[e - 2, owner]
        return pltpu.make_async_remote_copy(
            src_ref=ref, dst_ref=ref,
            send_sem=piece_send.at[e, j], recv_sem=piece_recv.at[e, j],
            device_id=(my_shot ^ hop, my_lag), device_id_type=MESH,
        )

    def lag_copy(e, j, delta, arriving=False):
        v = low_bit(delta)
        ref = full_v.at[my_lag ^ (delta if arriving else delta ^ v), e, my_shot ^ j]
        return pltpu.make_async_remote_copy(
            src_ref=ref, dst_ref=ref,
            send_sem=lag_send.at[e, j, delta], recv_sem=lag_recv.at[e, j, delta],
            device_id=(my_shot, my_lag ^ v), device_id_type=MESH,
        )

    def reduce(e):
        total = part_v[e, my_shot]
        for j in range(1, shot_shards):
            reduce_copy(e, j).wait_recv()
            total = total + recv_v[e, j]
        total = total * scales[0] * scales[1]
        if e < 2:
            full_v[my_lag, e, my_shot] = total
        else:
            rfull_v[e - 2, my_shot] = total
        for j in [*range(2, shot_shards, 2), 1]:
            piece_copy(e, j).start()

    def collect(e):
        for j in range(2, shot_shards, 2):
            piece_copy(e, j, True).wait_recv()
            piece_copy(e, j | 1).start()

    def share(e, collected):
        for j in [*range(0, shot_shards, 2), *range(1, shot_shards, 2)]:
            if j % 2 or (j and not collected):
                piece_copy(e, j, True).wait_recv()
            if j and j % 2 == 0 and not collected:
                piece_copy(e, j | 1).start()
            for v in bits:
                lag_copy(e, j, v).start()

    def relay(e):
        for j in range(shot_shards):
            for delta in deltas:
                if low_bit(delta) > 1:
                    lag_copy(e, j, delta, True).wait_recv()
                    for v in bits:
                        if v < low_bit(delta):
                            lag_copy(e, j, delta | v).start()

    def far_step(c, carry):
        forward(c, far)
        settle(c, far)
        correlate(c, 1, 1 - my_half)
        return carry

    def out_copy(c):
        return pltpu.make_async_copy(all_v.at[c], spec_ref.at[c], out_sem.at[c])

    scatter(0)
    lax.fori_loop(0, chunks - 1, far_step, 0)
    reduce(0)
    far_step(chunks - 1, 0)
    scatter(1)
    for c in range(chunks):
        out_copy(c).start()
    share(0, False)
    reduce(1)
    reduce(3)
    reduce(2)
    share(1, False)
    relay(0)
    collect(3)
    collect(2)
    relay(1)
    for e in (2, 3):
        for j in range(1, shot_shards, 2):
            piece_copy(e, j, True).wait_recv()
    unit = min(piece, local)
    for h in range(2):
        side = my_half if h == 0 else 1 - my_half
        lanes = pl.ds(pl.multiple_of(side * half, half), half)
        for p in range(shot_shards):
            for r in range(0, piece, unit):
                k, a = (p * piece + r) // local, (p * piece + r) % local
                rhs_ref[k, a : a + unit, lanes] = rfull_v[h, p, r : r + unit]
    for e in range(2):
        for j in range(shot_shards):
            for delta in deltas:
                if low_bit(delta) == 1:
                    lag_copy(e, j, delta, True).wait_recv()
    for q in range(lag_shards):
        for h in range(2):
            lane = ((q // (lag_shards // 2)) ^ h) * half
            for p in range(shot_shards):
                for r in range(0, piece, unit):
                    k, a = (p * piece + r) // local, (p * piece + r) % local + q * local
                    sys_ref[k, a : a + unit, lane : lane + half] = full_v[q, h, p, r : r + unit]
    for c in range(chunks):
        out_copy(c).wait()
        for delta in deltas:
            spec_copy(c, delta).wait_send()
    for e in range(4):
        for j in range(1, shot_shards):
            reduce_copy(e, j).wait_send()
            piece_copy(e, j).wait_send()
    for e in range(2):
        for j in range(shot_shards):
            for delta in deltas:
                lag_copy(e, j, delta).wait_send()


def front(traces, table, live, cosine, sine, shot_shards, lag_shards):
    shots, local, samples = traces.shape
    rows = shots * local
    width = table.shape[1]
    chunks = width // (2 * FINE)
    channels = local * lag_shards
    half = channels // 2
    blocks = 4
    piece = LAGS * local // shot_shards
    total_shots = shots * shot_shards
    scales = (1.0 / samples, 1.0 / (samples * total_shots))
    hbm = pl.BlockSpec(memory_space=pltpu.HBM)
    vm = pl.BlockSpec(memory_space=pltpu.VMEM)
    sem = pltpu.SemaphoreType.DMA
    return pl.pallas_call(
        functools.partial(front_kernel, (shots, shot_shards, lag_shards), scales),
        out_shape=(
            jax.ShapeDtypeStruct((chunks, channels, shots * 2 * FINE), jnp.bfloat16),
            jax.ShapeDtypeStruct((LAGS, channels, channels), jnp.float32),
            jax.ShapeDtypeStruct((LAGS, local, channels), jnp.float32),
        ),
        in_specs=[hbm, hbm, vm, vm, vm],
        out_specs=(hbm, vm, vm),
        scratch_shapes=[
            pltpu.VMEM((2 * rows, samples // 2), jnp.bfloat16),
            pltpu.VMEM((chunks, samples // 2, 2 * FINE), jnp.bfloat16),
            pltpu.VMEM((chunks, channels, shots * 2 * FINE), jnp.bfloat16),
            pltpu.VMEM((chunks, 2 * LAGS * local, shots * 2 * FINE), jnp.bfloat16),
            pltpu.VMEM((2, 2 * LAGS * local, half), jnp.float32),
            pltpu.VMEM((4, shot_shards, piece, half), jnp.float32),
            pltpu.VMEM((4, shot_shards, piece, half), jnp.float32),
            pltpu.VMEM((lag_shards, 2, shot_shards, piece, half), jnp.float32),
            pltpu.VMEM((2, shot_shards, piece, half), jnp.float32),
            sem((blocks, 2)),
            sem((chunks + blocks,)),
            sem((chunks,)),
            sem((chunks, lag_shards)),
            sem((chunks, lag_shards)),
            sem((4, shot_shards)),
            sem((4, shot_shards)),
            sem((4, shot_shards)),
            sem((4, shot_shards)),
            sem((2, shot_shards, lag_shards)),
            sem((2, shot_shards, lag_shards)),
        ],
        compiler_params=pltpu.CompilerParams(
            collective_id=0, has_side_effects=True, vmem_limit_bytes=56 << 20
        ),
        name="front",
    )(traces.reshape(rows, samples), table, live, cosine, sine)


def tail_kernel(
    shots, scale, spec_hbm, filter_ref, cos_ref, sin_ref, live_ref, table_hbm, out_hbm,
    spec_v, tab_v, err_v, stage_v, spec_sem, tab_sem, out_sem,
):
    chunks, channels = spec_v.shape[:2]
    local = filter_ref.shape[0]
    rows = shots * local
    wide = 2 * FINE
    steps, step = tab_v.shape[:2]
    my_lag = lax.axis_index("lag")

    def spec_copy(c):
        return pltpu.make_async_copy(spec_hbm.at[c], spec_v.at[c], spec_sem.at[c])

    def table_copy(t):
        span = pl.ds(pl.multiple_of(t * step, step), step)
        return pltpu.make_async_copy(table_hbm.at[span], tab_v.at[t], tab_sem.at[t])

    def out_copy(t, side):
        span = pl.ds(pl.multiple_of((side * steps + t) * step, step), step)
        slot = lax.rem(t, 2)
        return pltpu.make_async_copy(
            stage_v.at[slot, pl.ds(side * rows, rows)], out_hbm.at[:, span], out_sem.at[slot, side]
        )

    for c in range(chunks):
        spec_copy(c).start()
    taps = jnp.concatenate(
        [filter_ref[:, j * channels : (j + 1) * channels] for j in range(LAGS)], axis=0
    )
    for c in range(chunks):
        spec_copy(c).wait()
        if c == chunks // 2:
            for t in range(steps):
                table_copy(t).start()
        own = spec_v[c, pl.ds(pl.multiple_of(my_lag * local, local), local), :].astype(jnp.float32)
        turn_cos, turn_sin = quarter_turn(c, (1, FINE))
        for s in range(shots):
            o = s * wide
            mixed = jnp.dot(taps, spec_v[c, :, o : o + wide], preferred_element_type=jnp.float32)
            real, imag = own[:, o : o + FINE], own[:, o + FINE : o + wide]
            for j in range(LAGS):
                cosine, sine = cos_ref[c, LAGS + j : LAGS + j + 1, :], sin_ref[c, LAGS + j : LAGS + j + 1, :]
                a = mixed[j * local : (j + 1) * local, :FINE]
                b = mixed[j * local : (j + 1) * local, FINE:]
                real = real - (a * cosine - b * sine)
                imag = imag - (b * cosine + a * sine)
            top, lane = s * local, c * wide
            err_v[top : top + local, lane : lane + FINE] = real.astype(jnp.bfloat16)
            err_v[top : top + local, lane + FINE : lane + wide] = imag.astype(jnp.bfloat16)
            top = rows + top
            err_v[top : top + local, lane : lane + FINE] = (real * turn_cos + imag * turn_sin).astype(jnp.bfloat16)
            err_v[top : top + local, lane + FINE : lane + wide] = (imag * turn_cos - real * turn_sin).astype(jnp.bfloat16)
    live = live_ref[...].astype(jnp.float32).T * scale
    live = jnp.concatenate([live[:, s : s + 1] for s in range(shots)], axis=0)

    def back_step(t, carry):
        table_copy(t).wait()

        @pl.when(t >= 2)
        def _():
            for side in range(2):
                out_copy(t - 2, side).wait()

        value = lax.dot_general(
            err_v[...], tab_v[t], (((1,), (1,)), ((), ())), preferred_element_type=jnp.float32
        )
        slot = lax.rem(t, 2)
        for side in range(2):
            stage_v[slot, side * rows : (side + 1) * rows, :] = (
                value[side * rows : (side + 1) * rows] * live
            ).astype(jnp.bfloat16)
            out_copy(t, side).start()
        return carry

    lax.fori_loop(0, steps, back_step, 0)
    for t in range(max(steps - 2, 0), steps):
        for side in range(2):
            out_copy(t, side).wait()


def tail(all_spec, filter_rows, cosine, sine, live, table, shots):
    samples, depth = table.shape
    rows = live.size
    step = min(512, samples)
    hbm = pl.BlockSpec(memory_space=pltpu.HBM)
    vm = pl.BlockSpec(memory_space=pltpu.VMEM)
    return pl.pallas_call(
        functools.partial(tail_kernel, shots, 0.5 / samples),
        out_shape=jax.ShapeDtypeStruct((rows, 2 * samples), jnp.bfloat16),
        in_specs=[hbm, vm, vm, vm, vm, hbm],
        out_specs=hbm,
        scratch_shapes=[
            pltpu.VMEM(all_spec.shape, jnp.bfloat16),
            pltpu.VMEM((samples // step, step, depth), jnp.bfloat16),
            pltpu.VMEM((2 * rows, depth), jnp.bfloat16),
            pltpu.VMEM((2, 2 * rows, step), jnp.bfloat16),
            pltpu.SemaphoreType.DMA((all_spec.shape[0],)),
            pltpu.SemaphoreType.DMA((samples // step,)),
            pltpu.SemaphoreType.DMA((2, 2)),
        ],
        compiler_params=pltpu.CompilerParams(vmem_limit_bytes=62 << 20),
        name="tail",
    )(all_spec, filter_rows, cosine, sine, live, table)


def delay_tables(delays, samples, band_size):
    harmonic = jnp.arange(1, band_size + 1, dtype=jnp.int32)
    phase = delays[:, None] * harmonic[None, :] % (2 * samples)
    angle = phase.astype(jnp.float32) * (jnp.pi / samples)
    return (jnp.cos(angle), jnp.sin(angle))


def shards(traces, live_mask, gap_samples):
    shot_count, local_chan, samples = traces.shape
    band_size = samples // 16
    shot_shards, lag_shards = lax.axis_size("shot"), lax.axis_size("lag")
    table = jnp.asarray(dft_table(samples, band_size))
    spacing = samples // (2 * band_size)
    tap_delays = jnp.arange(LAGS, dtype=jnp.int32) * spacing
    lag_list = jnp.concatenate([tap_delays, gap_samples[0] + tap_delays])
    cosine, sine = delay_tables(lag_list, samples, band_size)

    def by_chunk(x):
        return x.reshape(2 * LAGS, band_size // FINE, FINE).transpose(1, 0, 2)

    cosine, sine = by_chunk(cosine), by_chunk(sine)
    turn = jnp.where(jnp.arange(2 * LAGS) < LAGS, 1.0, -1.0)[None, :, None]
    all_spec, system, rhs = front(traces, table, live_mask, cosine, sine * turn, shot_shards, lag_shards)
    filter_rows = solve(system, rhs)
    restored = tail(all_spec, filter_rows, cosine, sine, live_mask, table, shot_count)
    return restored.reshape(shot_count, local_chan, samples)


def solution(mesh):
    placed = (P("shot", "lag", None), P("shot", "lag"), P())
    return jax.shard_map(
        shards, mesh=mesh, in_specs=placed, out_specs=P("shot", "lag", None), check_vma=False
    )
```

```python
import functools

import jax
import jax.numpy as jnp
import ml_dtypes
import numpy as np
from jax import lax
from jax.experimental import pallas as pl
from jax.experimental.pallas import tpu as pltpu
from jax.sharding import PartitionSpec as P

LAGS=4
HALF=128
STEP=8

def mm(a, b, dims=((1,), (0,))):
    return lax.dot_general(a, b, (dims, ((), ())), precision=lax.Precision.HIGHEST, preferred_element_type=jnp.float32)


def spread(x):
    return jnp.broadcast_to(x, (STEP, HALF))


def lane_columns(tile, first):
    return [
        jnp.take_along_axis(tile, jnp.full(tile.shape, first + j, jnp.int32), axis=1) for j in range(STEP)
    ]


def row_of(tile, i):
    return spread(tile[i : i + 1, :])


def tree_sum(terms):
    while len(terms) > 1:
        terms = [terms[i] + terms[i + 1] for i in range(0, len(terms), 2)]
    return terms[0]


def factor_half(mat):
    lane = lax.broadcasted_iota(jnp.int32, (STEP, HALF), 1)
    row = lax.broadcasted_iota(jnp.int32, (STEP, HALF), 0)
    count = HALF // STEP
    tiles = [mat[STEP * t : STEP * t + STEP, :] for t in range(count)]
    pivot_cols = lane_columns(tiles[0], 0)
    cols = {t: lane_columns(tiles[t], 0) for t in range(1, count)}
    ahead = lane_columns(tiles[1], STEP)
    done = []
    for h in range(count):
        k = STEP * h
        last = h == count - 1
        inside = (lane >= k) & (lane < k + STEP)
        p = {(i, j): row_of(pivot_cols[i], j) for i in range(STEP) for j in range(i, STEP)}
        u = [jnp.where(inside, jnp.where(lane == k + i, 1.0, 0.0), row_of(tiles[h], i)) for i in range(STEP)]
        low, inv, root = {}, [None] * STEP, [None] * STEP
        for i in range(STEP):
            root[i] = lax.rsqrt(p[i, i])
            inv[i] = root[i] * root[i]
            for j in range(i + 1, STEP):
                low[j, i] = p[i, j] * inv[i]
            for j in range(i + 1, STEP):
                for m in range(j, STEP):
                    p[j, m] = p[j, m] - low[j, i] * p[i, m]
            for j in range(i + 1, STEP):
                u[j] = u[j] - low[j, i] * u[i]
                if not last:
                    cols[h + 1][j] = cols[h + 1][j] - low[j, i] * cols[h + 1][i]
        final = u[0] * root[0]
        for i in range(1, STEP):
            final = jnp.where(row == i, u[i] * root[i], final)
        done.append(jnp.where(lane <= row + k, final, 0.0))
        if last:
            break
        scaled = [cols[h + 1][m] * inv[m] for m in range(STEP)]
        pivot_cols = [
            ahead[j] - tree_sum([scaled[m] * row_of(cols[h + 1][m], j) for m in range(STEP)])
            for j in range(STEP)
        ]
        v = [u[i] * inv[i] for i in range(STEP)]
        for t in range(h + 1, count):
            if t > h + 1:
                for i in range(STEP):
                    for j in range(i + 1, STEP):
                        cols[t][j] = cols[t][j] - low[j, i] * cols[t][i]
            update = tree_sum([cols[t][j] * v[j] for j in range(STEP)])
            tiles[t] = jnp.where(inside, 0.0, tiles[t]) - update
            if t > h + 1:
                cols[t] = lane_columns(tiles[t], k + STEP)
            if t == h + 2:
                ahead = lane_columns(tiles[t], k + 2 * STEP)
    return jnp.concatenate(done, axis=0)


def solve_kernel(corr_hbm, rhs_hbm, out_ref, aug, diag, first_inv, coupling, zero_v, load_sem):
    channels = corr_hbm.shape[1]
    order = LAGS * channels
    block = 2 * HALF
    count = order // block
    local = rhs_hbm.shape[1]

    zero_copy = pltpu.make_async_copy(corr_hbm.at[0], zero_v, load_sem.at[0])
    zero_copy.start()
    loads = []
    for lag in range(1, LAGS):
        for low in range(LAGS - lag):
            rows, cols = (low + lag) * channels, low * channels
            loads.append((corr_hbm.at[lag], aug.at[pl.ds(rows, channels), pl.ds(cols, channels)]))
    for tap in range(LAGS):
        loads.append((rhs_hbm.at[tap], aug.at[pl.ds(order, local), pl.ds(tap * channels, channels)]))
    loads = [
        pltpu.make_async_copy(source, target, load_sem.at[1 + i]) for i, (source, target) in enumerate(loads)
    ]
    for load in loads:
        load.start()
    zero_copy.wait()
    value = zero_v[...]
    same = lax.broadcasted_iota(jnp.int32, value.shape, 0) == lax.broadcasted_iota(jnp.int32, value.shape, 1)
    trace = jnp.sum(jnp.where(same, value, 0.0))
    value = value + jnp.where(same, 0.1 * (trace / channels) + 1e-06, 0.0)
    for tap in range(LAGS):
        span = slice(tap * channels, (tap + 1) * channels)
        aug[span, span] = value
    diag[...] = value[:HALF, :HALF]

    def step(half_step, carry):
        diag[...] = factor_half(diag[...])
        for b in range(count):
            o = b * block
            mid, end = o + HALF, o + block

            @pl.when(half_step == 2 * b)
            def _():
                low = mm(aug[mid:end, o:mid], diag[...], ((1,), (1,)))
                first_inv[...] = diag[...]
                coupling[...] = low
                diag[...] = aug[mid:end, mid:end] - mm(low, low, ((1,), (1,)))

            @pl.when(half_step == 2 * b + 1)
            def _():
                if b == 0:
                    for load in loads:
                        load.wait()
                top, last = first_inv[...], diag[...]
                aug[o:mid, o:mid] = top
                aug[o:mid, mid:end] = jnp.zeros((HALF, HALF), jnp.float32)
                aug[mid:end, o:mid] = -mm(last, mm(coupling[...], top))
                aug[mid:end, mid:end] = last
                aug[end:, o:end] = mm(aug[end:, o:end], aug[o:end, o:end], ((1,), (1,)))
                for c in range(end, order, block):
                    aug[c:, c : c + block] = aug[c:, c : c + block] - mm(
                        aug[c:, o:end], aug[c : c + block, o:end], ((1,), (1,))
                    )
                if end < order:
                    diag[...] = aug[end : end + HALF, end : end + HALF]

        return carry

    lax.fori_loop(0, 2 * count, step, 0)
    for b in range(count - 1, -1, -1):
        o, end = b * block, (b + 1) * block
        known = aug[order:, o:end]
        if end < order:
            known = known - mm(aug[order:, end:order], aug[end:order, o:end])
        aug[order:, o:end] = mm(known, aug[o:end, o:end])
    out_ref[...] = aug[order:, :].astype(jnp.bfloat16)


def solve(corr, rhs):
    channels = corr.shape[1]
    local = rhs.shape[1]
    order = LAGS * channels
    vm = pl.BlockSpec(memory_space=pltpu.VMEM)
    hbm = pl.BlockSpec(memory_space=pltpu.HBM)
    return pl.pallas_call(
        solve_kernel,
        out_shape=jax.ShapeDtypeStruct((local, order), jnp.bfloat16),
        in_specs=[hbm, hbm],
        out_specs=vm,
        scratch_shapes=[
            pltpu.VMEM((order + local, order), jnp.float32),
            pltpu.VMEM((HALF, HALF), jnp.float32),
            pltpu.VMEM((HALF, HALF), jnp.float32),
            pltpu.VMEM((HALF, HALF), jnp.float32),
            pltpu.VMEM((channels, channels), jnp.float32),
            pltpu.SemaphoreType.DMA((1 + LAGS * (LAGS - 1) // 2 + LAGS,)),
        ],
        compiler_params=pltpu.CompilerParams(vmem_limit_bytes=63 << 20),
        name="block_solve",
    )(corr, rhs)


MESH = pl.DeviceIdType.MESH
FINE = 128


def dft_table(samples, band_size):
    times = np.arange(samples // 2, dtype=np.int64)
    harmonic = np.arange(1, band_size + 1, dtype=np.int64)
    phase = (times[:, None] * harmonic[None, :]) % (2 * samples)
    circle = np.arange(2 * samples).astype(np.float32) * np.float32(np.pi / samples)
    cosines = np.cos(circle.astype(np.float64)).astype(np.float32).astype(ml_dtypes.bfloat16)[phase]
    sines = np.sin(circle.astype(np.float64)).astype(np.float32).astype(ml_dtypes.bfloat16)[phase]
    pair = np.stack([cosines.reshape(samples // 2, -1, FINE), sines.reshape(samples // 2, -1, FINE)], axis=2)
    return pair.reshape(samples // 2, 2 * band_size)


def low_bit(value):
    return value & -value


def quarter_turn(c, shape):
    harmonic = (lax.broadcasted_iota(jnp.int32, shape, 1) + (c * FINE + 1)) & 3
    cosine = jnp.where(harmonic == 0, 1.0, jnp.where(harmonic == 2, -1.0, 0.0))
    sine = jnp.where(harmonic == 1, 1.0, jnp.where(harmonic == 3, -1.0, 0.0))
    return cosine, sine


def front_kernel(
    shape, scales, x_hbm, table_hbm, live_ref, cos_ref, sin_ref, spec_ref, sys_ref, rhs_ref,
    x_v, tab_v, all_v, rot_v, acc_v, part_v, recv_v, full_v, rfull_v,
    x_sem, tab_sem, out_sem, spec_send, spec_recv, red_send, red_recv, piece_send, piece_recv, lag_send, lag_recv,
):
    shots, shot_shards, lag_shards = shape
    rows, samples = x_v.shape[0] // 2, x_v.shape[1]
    local = rows // shots
    chunks = all_v.shape[0]
    channels = all_v.shape[1]
    wide = 2 * FINE
    blocks = x_sem.shape[0]
    block = samples // blocks
    my_shot, my_lag = lax.axis_index("shot"), lax.axis_index("lag")
    bits = [1 << i for i in range(lag_shards.bit_length() - 2, -1, -1)]
    deltas = sorted(range(1, lag_shards), key=lambda d: -low_bit(d))
    near = [d for d in deltas if d < lag_shards // 2]
    far = [d for d in deltas if d >= lag_shards // 2]
    half = channels // 2
    my_half = my_lag // (lag_shards // 2)

    def x_copy(b, side):
        span = pl.ds(b * block, block)
        return pltpu.make_async_copy(
            x_hbm.at[:, pl.ds(side * samples + b * block, block)],
            x_v.at[pl.ds(side * rows, rows), span], x_sem.at[b, side],
        )

    def first_copy(b):
        span = pl.ds(b * block, block)
        return pltpu.make_async_copy(
            table_hbm.at[span, pl.ds(0, wide)], tab_v.at[0, span], tab_sem.at[chunks + b]
        )

    def table_copy(c):
        return pltpu.make_async_copy(
            table_hbm.at[:, pl.ds(pl.multiple_of(c * wide, wide), wide)], tab_v.at[c], tab_sem.at[c]
        )

    for b in range(blocks):
        first_copy(b).start()
        for side in range(2):
            x_copy(b, side).start()

    barrier = pltpu.get_barrier_semaphore()
    for j in range(1, shot_shards):
        pl.semaphore_signal(barrier, inc=1, device_id=(my_shot ^ j, my_lag), device_id_type=MESH)
    for v in bits:
        pl.semaphore_signal(barrier, inc=1, device_id=(my_shot, my_lag ^ v), device_id_type=MESH)

    def rows_of(lag):
        return pl.ds(pl.multiple_of(lag * local, local), local)

    def spec_copy(c, delta, arriving=False):
        v = low_bit(delta)
        span = rows_of(my_lag ^ (delta if arriving else delta ^ v))
        return pltpu.make_async_remote_copy(
            src_ref=all_v.at[c, span], dst_ref=all_v.at[c, span],
            send_sem=spec_send.at[c, delta], recv_sem=spec_recv.at[c, delta],
            device_id=(my_shot, my_lag ^ v), device_id_type=MESH,
        )

    def forward(c, group):
        for delta in group:
            if low_bit(delta) > 1:
                spec_copy(c, delta, True).wait_recv()
                for v in bits:
                    if v < low_bit(delta):
                        spec_copy(c, delta | v).start()

    def settle(c, group):
        for delta in group:
            if low_bit(delta) == 1:
                spec_copy(c, delta, True).wait_recv()

    def transform(c, loaded):
        total = None
        for b in range(blocks):
            if loaded is not None:
                loaded(b)
            term = jnp.dot(
                x_v[:, b * block : (b + 1) * block], tab_v[c, b * block : (b + 1) * block, :],
                preferred_element_type=jnp.float32,
            )
            total = term if total is None else total + term
        turn_cos, turn_sin = quarter_turn(c, (1, FINE))
        early, late = total[:rows], total[rows:]
        live = live_ref[...].astype(jnp.float32).T
        real = early[:, :FINE] + (late[:, :FINE] * turn_cos - late[:, FINE:] * turn_sin)
        imag = early[:, FINE:] + (late[:, FINE:] * turn_cos + late[:, :FINE] * turn_sin)
        for s in range(shots):
            span, o = slice(s * local, (s + 1) * local), s * wide
            all_v[c, rows_of(my_lag), o : o + FINE] = (real[span] * live[:, s : s + 1]).astype(jnp.bfloat16)
            all_v[c, rows_of(my_lag), o + FINE : o + wide] = (imag[span] * live[:, s : s + 1]).astype(jnp.bfloat16)

    def send_own(c):
        for v in bits:
            spec_copy(c, v).start()

    def rotate(c):
        own = all_v[c, rows_of(my_lag), :].astype(jnp.float32)
        for k in range(2 * LAGS):
            cosine, sine = cos_ref[c, k : k + 1, :], sin_ref[c, k : k + 1, :]
            for s in range(shots):
                o = s * wide
                real, imag = own[:, o : o + FINE], own[:, o + FINE : o + wide]
                rot_v[c, k * local : (k + 1) * local, o : o + FINE] = (real * cosine - imag * sine).astype(jnp.bfloat16)
                rot_v[c, k * local : (k + 1) * local, o + FINE : o + wide] = (imag * cosine + real * sine).astype(jnp.bfloat16)

    def correlate(c, h, side):
        acc_v[h] = acc_v[h] + lax.dot_general(
            rot_v[c], all_v[c, pl.ds(pl.multiple_of(side * half, half), half), :],
            (((1,), (1,)), ((), ())), preferred_element_type=jnp.float32,
        )

    def first_loaded(b):
        first_copy(b).wait()
        for side in range(2):
            x_copy(b, side).wait()
        if b + 1 == blocks:
            for c in range(1, chunks):
                table_copy(c).start()

    acc_v[...] = jnp.zeros_like(acc_v)
    transform(0, first_loaded)
    pl.semaphore_wait(barrier, shot_shards - 1 + len(bits))
    send_own(0)

    def transform_step(c, carry):
        table_copy(c).wait()
        rotate(c - 1)
        transform(c, None)
        send_own(c)
        return carry

    lax.fori_loop(1, chunks, transform_step, 0)
    rotate(chunks - 1)

    def near_step(c, carry):
        forward(c, near)
        settle(c, near)
        correlate(c, 0, my_half)
        return carry

    lax.fori_loop(0, chunks, near_step, 0)

    piece = part_v.shape[2]

    def reduce_copy(e, j):
        return pltpu.make_async_remote_copy(
            src_ref=part_v.at[e, my_shot ^ j], dst_ref=recv_v.at[e, j],
            send_sem=red_send.at[e, j], recv_sem=red_recv.at[e, j],
            device_id=(my_shot ^ j, my_lag), device_id_type=MESH,
        )

    def scatter(h):
        for g in range(2):
            for p in range(shot_shards):
                top = g * LAGS * local + p * piece
                part_v[2 * g + h, p] = acc_v[h, top : top + piece, :]
        for g in range(2):
            for j in range(1, shot_shards):
                reduce_copy(2 * g + h, j).start()

    def piece_copy(e, j, arriving=False):
        hop = 1 if j % 2 else j
        owner = my_shot ^ (j if arriving else j ^ hop)
        ref = full_v.at[my_lag, e, owner] if e < 2 else rfull_v.at[e - 2, owner]
        return pltpu.make_async_remote_copy(
            src_ref=ref, dst_ref=ref,
            send_sem=piece_send.at[e, j], recv_sem=piece_recv.at[e, j],
            device_id=(my_shot ^ hop, my_lag), device_id_type=MESH,
        )

    def lag_copy(e, j, delta, arriving=False):
        v = low_bit(delta)
        ref = full_v.at[my_lag ^ (delta if arriving else delta ^ v), e, my_shot ^ j]
        return pltpu.make_async_remote_copy(
            src_ref=ref, dst_ref=ref,
            send_sem=lag_send.at[e, j, delta], recv_sem=lag_recv.at[e, j, delta],
            device_id=(my_shot, my_lag ^ v), device_id_type=MESH,
        )

    def reduce(e):
        total = part_v[e, my_shot]
        for j in range(1, shot_shards):
            reduce_copy(e, j).wait_recv()
            total = total + recv_v[e, j]
        total = total * scales[0] * scales[1]
        if e < 2:
            full_v[my_lag, e, my_shot] = total
        else:
            rfull_v[e - 2, my_shot] = total
        for j in [*range(2, shot_shards, 2), 1]:
            piece_copy(e, j).start()

    def collect(e):
        for j in range(2, shot_shards, 2):
            piece_copy(e, j, True).wait_recv()
            piece_copy(e, j | 1).start()

    def share(e, collected):
        for j in [*range(0, shot_shards, 2), *range(1, shot_shards, 2)]:
            if j % 2 or (j and not collected):
                piece_copy(e, j, True).wait_recv()
            if j and j % 2 == 0 and not collected:
                piece_copy(e, j | 1).start()
            for v in bits:
                lag_copy(e, j, v).start()

    def relay(e):
        for j in range(shot_shards):
            for delta in deltas:
                if low_bit(delta) > 1:
                    lag_copy(e, j, delta, True).wait_recv()
                    for v in bits:
                        if v < low_bit(delta):
                            lag_copy(e, j, delta | v).start()

    def far_step(c, carry):
        forward(c, far)
        settle(c, far)
        correlate(c, 1, 1 - my_half)
        return carry

    def out_copy(c):
        return pltpu.make_async_copy(all_v.at[c], spec_ref.at[c], out_sem.at[c])

    scatter(0)
    lax.fori_loop(0, chunks - 1, far_step, 0)
    reduce(0)
    far_step(chunks - 1, 0)
    scatter(1)
    for c in range(chunks):
        out_copy(c).start()
    share(0, False)
    reduce(1)
    reduce(3)
    reduce(2)
    relay(0)
    share(1, False)
    collect(3)
    collect(2)
    relay(1)
    for e in (2, 3):
        for j in range(1, shot_shards, 2):
            piece_copy(e, j, True).wait_recv()
    unit = min(piece, local)
    for h in range(2):
        side = my_half if h == 0 else 1 - my_half
        lanes = pl.ds(pl.multiple_of(side * half, half), half)
        for p in range(shot_shards):
            for r in range(0, piece, unit):
                k, a = (p * piece + r) // local, (p * piece + r) % local
                rhs_ref[k, a : a + unit, lanes] = rfull_v[h, p, r : r + unit]
    for e in range(2):
        for j in range(shot_shards):
            for delta in deltas:
                if low_bit(delta) == 1:
                    lag_copy(e, j, delta, True).wait_recv()
    for q in range(lag_shards):
        for h in range(2):
            lane = ((q // (lag_shards // 2)) ^ h) * half
            for p in range(shot_shards):
                for r in range(0, piece, unit):
                    k, a = (p * piece + r) // local, (p * piece + r) % local + q * local
                    sys_ref[k, a : a + unit, lane : lane + half] = full_v[q, h, p, r : r + unit]
    for c in range(chunks):
        out_copy(c).wait()
        for delta in deltas:
            spec_copy(c, delta).wait_send()
    for e in range(4):
        for j in range(1, shot_shards):
            reduce_copy(e, j).wait_send()
            piece_copy(e, j).wait_send()
    for e in range(2):
        for j in range(shot_shards):
            for delta in deltas:
                lag_copy(e, j, delta).wait_send()


def front(traces, table, live, cosine, sine, shot_shards, lag_shards):
    shots, local, samples = traces.shape
    rows = shots * local
    width = table.shape[1]
    chunks = width // (2 * FINE)
    channels = local * lag_shards
    half = channels // 2
    blocks = 4
    piece = LAGS * local // shot_shards
    total_shots = shots * shot_shards
    scales = (1.0 / samples, 1.0 / (samples * total_shots))
    hbm = pl.BlockSpec(memory_space=pltpu.HBM)
    vm = pl.BlockSpec(memory_space=pltpu.VMEM)
    sem = pltpu.SemaphoreType.DMA
    return pl.pallas_call(
        functools.partial(front_kernel, (shots, shot_shards, lag_shards), scales),
        out_shape=(
            jax.ShapeDtypeStruct((chunks, channels, shots * 2 * FINE), jnp.bfloat16),
            jax.ShapeDtypeStruct((LAGS, channels, channels), jnp.float32),
            jax.ShapeDtypeStruct((LAGS, local, channels), jnp.float32),
        ),
        in_specs=[hbm, hbm, vm, vm, vm],
        out_specs=(hbm, vm, vm),
        scratch_shapes=[
            pltpu.VMEM((2 * rows, samples // 2), jnp.bfloat16),
            pltpu.VMEM((chunks, samples // 2, 2 * FINE), jnp.bfloat16),
            pltpu.VMEM((chunks, channels, shots * 2 * FINE), jnp.bfloat16),
            pltpu.VMEM((chunks, 2 * LAGS * local, shots * 2 * FINE), jnp.bfloat16),
            pltpu.VMEM((2, 2 * LAGS * local, half), jnp.float32),
            pltpu.VMEM((4, shot_shards, piece, half), jnp.float32),
            pltpu.VMEM((4, shot_shards, piece, half), jnp.float32),
            pltpu.VMEM((lag_shards, 2, shot_shards, piece, half), jnp.float32),
            pltpu.VMEM((2, shot_shards, piece, half), jnp.float32),
            sem((blocks, 2)),
            sem((chunks + blocks,)),
            sem((chunks,)),
            sem((chunks, lag_shards)),
            sem((chunks, lag_shards)),
            sem((4, shot_shards)),
            sem((4, shot_shards)),
            sem((4, shot_shards)),
            sem((4, shot_shards)),
            sem((2, shot_shards, lag_shards)),
            sem((2, shot_shards, lag_shards)),
        ],
        compiler_params=pltpu.CompilerParams(
            collective_id=0, has_side_effects=True, vmem_limit_bytes=56 << 20
        ),
        name="front",
    )(traces.reshape(rows, samples), table, live, cosine, sine)


def tail_kernel(
    shots, scale, spec_hbm, filter_ref, cos_ref, sin_ref, live_ref, table_hbm, out_hbm,
    spec_v, tab_v, err_v, stage_v, spec_sem, tab_sem, out_sem,
):
    chunks, channels = spec_v.shape[:2]
    local = filter_ref.shape[0]
    rows = shots * local
    wide = 2 * FINE
    steps, step = tab_v.shape[:2]
    my_lag = lax.axis_index("lag")

    def spec_copy(c):
        return pltpu.make_async_copy(spec_hbm.at[c], spec_v.at[c], spec_sem.at[c])

    def table_copy(t):
        span = pl.ds(pl.multiple_of(t * step, step), step)
        return pltpu.make_async_copy(table_hbm.at[span], tab_v.at[t], tab_sem.at[t])

    def out_copy(t, side):
        span = pl.ds(pl.multiple_of((side * steps + t) * step, step), step)
        slot = lax.rem(t, 2)
        return pltpu.make_async_copy(
            stage_v.at[slot, pl.ds(side * rows, rows)], out_hbm.at[:, span], out_sem.at[slot, side]
        )

    for c in range(chunks):
        spec_copy(c).start()
    taps = jnp.concatenate(
        [filter_ref[:, j * channels : (j + 1) * channels] for j in range(LAGS)], axis=0
    )
    for c in range(chunks):
        spec_copy(c).wait()
        if c == min(1, chunks - 1):
            for t in range(steps):
                table_copy(t).start()
        own = spec_v[c, pl.ds(pl.multiple_of(my_lag * local, local), local), :].astype(jnp.float32)
        turn_cos, turn_sin = quarter_turn(c, (1, FINE))
        for s in range(shots):
            o = s * wide
            mixed = jnp.dot(taps, spec_v[c, :, o : o + wide], preferred_element_type=jnp.float32)
            real, imag = own[:, o : o + FINE], own[:, o + FINE : o + wide]
            for j in range(LAGS):
                cosine, sine = cos_ref[c, LAGS + j : LAGS + j + 1, :], sin_ref[c, LAGS + j : LAGS + j + 1, :]
                a = mixed[j * local : (j + 1) * local, :FINE]
                b = mixed[j * local : (j + 1) * local, FINE:]
                real = real - (a * cosine - b * sine)
                imag = imag - (b * cosine + a * sine)
            top, lane = s * local, c * wide
            err_v[top : top + local, lane : lane + FINE] = real.astype(jnp.bfloat16)
            err_v[top : top + local, lane + FINE : lane + wide] = imag.astype(jnp.bfloat16)
            top = rows + top
            err_v[top : top + local, lane : lane + FINE] = (real * turn_cos + imag * turn_sin).astype(jnp.bfloat16)
            err_v[top : top + local, lane + FINE : lane + wide] = (imag * turn_cos - real * turn_sin).astype(jnp.bfloat16)
    live = live_ref[...].astype(jnp.float32).T * scale
    live = jnp.concatenate([live[:, s : s + 1] for s in range(shots)], axis=0)

    def back_step(t, carry):
        table_copy(t).wait()

        @pl.when(t >= 2)
        def _():
            for side in range(2):
                out_copy(t - 2, side).wait()

        value = lax.dot_general(
            err_v[...], tab_v[t], (((1,), (1,)), ((), ())), preferred_element_type=jnp.float32
        )
        slot = lax.rem(t, 2)
        for side in range(2):
            stage_v[slot, side * rows : (side + 1) * rows, :] = (
                value[side * rows : (side + 1) * rows] * live
            ).astype(jnp.bfloat16)
            out_copy(t, side).start()
        return carry

    lax.fori_loop(0, steps, back_step, 0)
    for t in range(max(steps - 2, 0), steps):
        for side in range(2):
            out_copy(t, side).wait()


def tail(all_spec, filter_rows, cosine, sine, live, table, shots):
    samples, depth = table.shape
    rows = live.size
    step = min(1024, samples)
    hbm = pl.BlockSpec(memory_space=pltpu.HBM)
    vm = pl.BlockSpec(memory_space=pltpu.VMEM)
    return pl.pallas_call(
        functools.partial(tail_kernel, shots, 0.5 / samples),
        out_shape=jax.ShapeDtypeStruct((rows, 2 * samples), jnp.bfloat16),
        in_specs=[hbm, vm, vm, vm, vm, hbm],
        out_specs=hbm,
        scratch_shapes=[
            pltpu.VMEM(all_spec.shape, jnp.bfloat16),
            pltpu.VMEM((samples // step, step, depth), jnp.bfloat16),
            pltpu.VMEM((2 * rows, depth), jnp.bfloat16),
            pltpu.VMEM((2, 2 * rows, step), jnp.bfloat16),
            pltpu.SemaphoreType.DMA((all_spec.shape[0],)),
            pltpu.SemaphoreType.DMA((samples // step,)),
            pltpu.SemaphoreType.DMA((2, 2)),
        ],
        compiler_params=pltpu.CompilerParams(vmem_limit_bytes=62 << 20),
        name="tail",
    )(all_spec, filter_rows, cosine, sine, live, table)


def delay_tables(delays, samples, band_size):
    harmonic = jnp.arange(1, band_size + 1, dtype=jnp.int32)
    phase = delays[:, None] * harmonic[None, :] % (2 * samples)
    angle = phase.astype(jnp.float32) * (jnp.pi / samples)
    return (jnp.cos(angle), jnp.sin(angle))


def shards(traces, live_mask, gap_samples):
    shot_count, local_chan, samples = traces.shape
    band_size = samples // 16
    shot_shards, lag_shards = lax.axis_size("shot"), lax.axis_size("lag")
    table = jnp.asarray(dft_table(samples, band_size))
    spacing = samples // (2 * band_size)
    tap_delays = jnp.arange(LAGS, dtype=jnp.int32) * spacing
    lag_list = jnp.concatenate([tap_delays, gap_samples[0] + tap_delays])
    cosine, sine = delay_tables(lag_list, samples, band_size)

    def by_chunk(x):
        return x.reshape(2 * LAGS, band_size // FINE, FINE).transpose(1, 0, 2)

    cosine, sine = by_chunk(cosine), by_chunk(sine)
    turn = jnp.where(jnp.arange(2 * LAGS) < LAGS, 1.0, -1.0)[None, :, None]
    all_spec, system, rhs = front(traces, table, live_mask, cosine, sine * turn, shot_shards, lag_shards)
    filter_rows = solve(system, rhs)
    restored = tail(all_spec, filter_rows, cosine, sine, live_mask, table, shot_count)
    return restored.reshape(shot_count, local_chan, samples)


def solution(mesh):
    placed = (P("shot", "lag", None), P("shot", "lag"), P())
    return jax.shard_map(
        shards, mesh=mesh, in_specs=placed, out_specs=P("shot", "lag", None), check_vma=False
    )
```
